128 devices in a mesh: seq: 32 (over z, y, core), dp: 4 (over x).
Axes of the slice: x: 4, y: 4, z: 4, core: 2. Of those that a mesh axis runs over, the one named last changes fastest.
Arguments:
- resid: bfloat16 [4, 16384, 2048], P('dp', 'seq'), may hold values from -6 to 6
- token_ids: int32 [4, 16384], P('dp', 'seq'), may hold values from 0 to 63999
- code_proj: float32 [6, 2048], replicated, may hold values from -2.5 to 2.5
- w_query: bfloat16 [2048, 1024], replicated, may hold values from -0.125 to 0.125
- w_key: bfloat16 [2048, 1024], replicated, may hold values from -0.125 to 0.125
- w_value: bfloat16 [2048, 1024], replicated, may hold values from -0.125 to 0.125
- gain: float32 [1024], replicated, may hold values from 0.1 to 1.9
- out_grad: bfloat16 [4, 16384, 1024], P('dp', 'seq'), may hold values from -6 to 6
Outputs:
- resid_grad: bfloat16 [4, 16384, 2048], P('dp', 'seq')
- weight_grads: float32 [2048, 3, 1024], P(('seq', 'dp'))
- gain_grad: float32 [1024], replicated
- code_grad: float32 [6, 2048], replicated
The draws below stay inside these ranges and needn't reach their ends.
Inputs may be any that keep to these rules, and one draw needn't show every extreme that they name: `token_ids`: ids of the codebook of 64000 codes.
All inputs are finite; a program needn't handle non-finite values.
Results may differ from the reference program's by a relative error of at most 0.0084.
Values sent between devices are 32-bit elements; how exact they have to be, the bound alone decides.
A program may use at most 128 MiB of HBM per device.

```python
import math
import jax
import jax.numpy as jnp
import numpy as np
from jax import lax

D = 2048
HEADS = 8
DH = 128
HD = 1024
CODES = 6
VOCAB = 64000
TOK_DEV = 512
SEQ_LEN = 16384
BATCH = 4
N_SEQ = 32


def plant(values, key, smallest, high):
    place = [jax.random.randint(jax.random.fold_in(key, axis), (), 0, length) for axis, length in enumerate(values.shape)]
    main_axis = values.shape.index(max(values.shape))
    next_to = place[:main_axis] + [(place[main_axis] + 1) % values.shape[main_axis]] + place[main_axis + 1:]
    return values.at[tuple(place)].set(smallest).at[tuple(next_to)].set(high)


def level_of(stream_key, dims, split, least, top_value):
    def one(axis_at, parts):
        draws = jax.random.uniform(jax.random.fold_in(jax.random.fold_in(stream_key, 6), axis_at), (parts,), jnp.float32, least / len(split), top_value / len(split))
        return jnp.repeat(jnp.exp(draws), dims[axis_at] // parts).reshape((-1,) + (1,) * (len(dims) - axis_at - 1))

    factor_of = one(*split[0])
    for cut in split[1:]:
        factor_of = factor_of * one(*cut)
    return factor_of


def rank_table(amount, skew):
    loads = [(1 << 20) // math.isqrt(grade ** skew) + 1 for grade in range(1, amount + 1)]
    deviation = 1 + sum(loads) // (1 << 30)
    return np.cumsum(np.array([max(1, weight // deviation) for weight in loads]))


def ranked(own_key, shape, count, slope):
    grid = rank_table(count, slope)
    ticket = jax.random.randint(jax.random.fold_in(own_key, 1), shape, 0, int(grid[count - 1]))
    grade = jnp.searchsorted(jnp.asarray(grid, jnp.int32), ticket, side="right")
    return jax.random.permutation(jax.random.fold_in(own_key, 2), count)[grade].astype(jnp.int32)


def centred(rng, dims, scale, limit, shards=(), dtype=jnp.bfloat16):
    entries = scale * jax.random.normal(rng, dims, jnp.float32)
    if shards:
        entries = entries * level_of(rng, dims, shards, -0.22, 0.18)
    return jnp.clip(entries, -limit, limit).astype(dtype)


def setup_inputs(seed: int = 0) -> dict:
    streams_of = jax.random.split(jax.random.key(seed), 9)
    return {
        "resid": centred(streams_of[0], (BATCH, SEQ_LEN, D), 1.0, 6.0, ((0, 4), (1, 32))),
        "token_ids": plant(ranked(streams_of[1], (BATCH, SEQ_LEN), VOCAB, 2), jax.random.fold_in(streams_of[1], 3), 0, VOCAB - 1).astype(jnp.int32),
        "code_proj": centred(streams_of[2], (CODES, D), CODES ** -0.5, 2.5, (), jnp.float32),
        "w_query": centred(streams_of[3], (D, HD), D ** -0.5, 0.125),
        "w_key": centred(streams_of[4], (D, HD), D ** -0.5, 0.125),
        "w_value": centred(streams_of[5], (D, HD), D ** -0.5, 0.125),
        "gain": jnp.clip(1.0 + 0.18 * jax.random.normal(streams_of[6], (HD,), jnp.float32), 0.1, 1.9),
        "out_grad": centred(streams_of[7], (BATCH, SEQ_LEN, HD), 1.0, 6.0, ((0, 4), (1, 32))),
    }


fsq_levels = (8, 8, 8, 5, 5, 5)
fsq_bases = (1, 8, 64, 512, 2560, 12800)

def code_rows(token_ids):
    code_list = []
    for fsq_level, fsq_base in zip(fsq_levels, fsq_bases):
        fsq_digit = token_ids // fsq_base % fsq_level
        code_list.append((2.0 * fsq_digit.astype(jnp.float32) - (fsq_level - 1)) / (fsq_level - 1))
    return jnp.stack(code_list)

def silu_slope(value):
    sigma = jax.nn.sigmoid(value)
    return sigma * (1.0 + value * (1.0 - sigma))

def reference(resid, token_ids, code_proj, w_query, w_key, w_value, gain, out_grad):
    f32 = jnp.float32
    codes = code_rows(token_ids)
    summed = resid.astype(f32)
    for index in range(codes.shape[0]):
        summed = summed + codes[index][..., None] * code_proj[index]
    inputs = summed.astype(jnp.bfloat16).reshape(BATCH * SEQ_LEN, D)
    query_pre = jnp.dot(inputs, w_query, preferred_element_type=f32)
    key_pre = jnp.dot(inputs, w_key, preferred_element_type=f32)
    value_pre = jnp.dot(inputs, w_value, preferred_element_type=f32)

    def to_heads(array):
        return array.reshape(BATCH, N_SEQ, TOK_DEV, HEADS, DH).transpose(1, 0, 3, 2, 4)

    def from_heads(array):
        return array.transpose(1, 0, 3, 2, 4).reshape(BATCH * SEQ_LEN, HD)
    queries = to_heads(jax.nn.silu(query_pre).astype(jnp.bfloat16))
    keys = to_heads(jax.nn.silu(key_pre).astype(jnp.bfloat16))
    values = to_heads(value_pre.astype(jnp.bfloat16))
    grads_out = to_heads(out_grad)
    gain_heads = gain.reshape(HEADS, 1, DH)
    block_kv = jnp.einsum('cbhte,cbhtd->cbhed', keys.astype(f32), values.astype(f32))
    empty_state = jnp.zeros_like(block_kv[:1])
    prefix = jnp.concatenate([empty_state, jnp.cumsum(block_kv, axis=0)[:-1]], axis=0).astype(jnp.bfloat16)
    row_ids = lax.broadcasted_iota(jnp.int32, (TOK_DEV, TOK_DEV), 0)
    col_ids = lax.broadcasted_iota(jnp.int32, (TOK_DEV, TOK_DEV), 1)
    causal = col_ids <= row_ids

    def block_scores(query_blk, key_blk):
        raw = jnp.einsum('bhte,bhse->bhts', query_blk.astype(f32), key_blk.astype(f32))
        return jnp.where(causal, raw, 0.0).astype(jnp.bfloat16)

    def forward_block(operands):
        query_blk, key_blk, value_blk, prefix_blk, grad_blk = operands
        scores = block_scores(query_blk, key_blk)
        attended = jnp.einsum('bhts,bhsd->bhtd', scores.astype(f32), value_blk.astype(f32))
        attended = attended + jnp.einsum('bhte,bhed->bhtd', query_blk.astype(f32), prefix_blk.astype(f32))
        root = jnp.sqrt(lax.optimization_barrier(jnp.mean(attended * attended, axis=-1, keepdims=True)) + 1e-06)
        normed = attended / root
        d_normed = grad_blk.astype(f32) * gain_heads
        d_att = ((d_normed - normed * lax.optimization_barrier(jnp.mean(d_normed * normed, axis=-1, keepdims=True))) / root).astype(jnp.bfloat16)
        gain_term = lax.optimization_barrier(jnp.sum(grad_blk.astype(f32) * normed, axis=2))
        return (d_att, gain_term)
    d_att, gain_terms = lax.map(forward_block, (queries, keys, values, prefix, grads_out))
    block_grad = jnp.einsum('cbhte,cbhtd->cbhed', queries.astype(f32), d_att.astype(f32))
    inclusive = jnp.flip(jnp.cumsum(jnp.flip(block_grad, axis=0), axis=0), axis=0)
    suffix = jnp.concatenate([inclusive[1:], empty_state], axis=0).astype(jnp.bfloat16)

    def backward_block(operands):
        query_blk, key_blk, value_blk, prefix_blk, suffix_blk, datt_blk = operands
        q32 = query_blk.astype(f32)
        k32 = key_blk.astype(f32)
        v32 = value_blk.astype(f32)
        a32 = datt_blk.astype(f32)
        p32 = prefix_blk.astype(f32)
        s32 = suffix_blk.astype(f32)
        scores = block_scores(query_blk, key_blk).astype(f32)
        back_scores = jnp.where(causal, jnp.einsum('bhtd,bhsd->bhts', a32, v32), 0.0).astype(jnp.bfloat16).astype(f32)
        d_query = jnp.einsum('bhts,bhse->bhte', back_scores, k32) + jnp.einsum('bhtd,bhed->bhte', a32, p32)
        d_key = jnp.einsum('bhts,bhte->bhse', back_scores, q32) + jnp.einsum('bhsd,bhed->bhse', v32, s32)
        d_value = jnp.einsum('bhts,bhtd->bhsd', scores, a32) + jnp.einsum('bhse,bhed->bhsd', k32, s32)
        return (d_query, d_key, d_value)
    d_query, d_key, d_value = lax.map(backward_block, (queries, keys, values, prefix, suffix, d_att))
    grad_q = (from_heads(d_query) * silu_slope(query_pre)).astype(jnp.bfloat16)
    grad_k = (from_heads(d_key) * silu_slope(key_pre)).astype(jnp.bfloat16)
    grad_v = from_heads(d_value).astype(jnp.bfloat16)
    transpose_dims = (((1,), (1,)), ((), ()))
    input_grad = lax.dot_general(grad_q, w_query, transpose_dims, preferred_element_type=f32)
    input_grad = input_grad + lax.dot_general(grad_k, w_key, transpose_dims, preferred_element_type=f32)
    input_grad = input_grad + lax.dot_general(grad_v, w_value, transpose_dims, preferred_element_type=f32)
    resid_grad = input_grad.astype(jnp.bfloat16).reshape(BATCH, SEQ_LEN, D)
    grad_scale = 1.0 / math.sqrt(BATCH * SEQ_LEN)
    row_dims = (((0,), (0,)), ((), ()))
    weight_grads = jnp.stack([lax.dot_general(inputs, grad_part, row_dims, preferred_element_type=f32) for grad_part in (grad_q, grad_k, grad_v)], axis=1) * grad_scale
    gain_grad = lax.optimization_barrier(jnp.sum(gain_terms, axis=(0, 1))).reshape(HD) * grad_scale
    code_grad = jnp.dot(codes.reshape(codes.shape[0], BATCH * SEQ_LEN), input_grad, precision=lax.Precision.HIGHEST) * grad_scale
    return (resid_grad, weight_grads, gain_grad, code_grad)
```

```python
import functools
import math

import jax
import jax.numpy as jnp
from jax import lax
from jax.experimental import pallas as pl
from jax.experimental.pallas import tpu as pltpu
from jax.sharding import Mesh
from jax.sharding import PartitionSpec as P

HEADS = 8
DH = 128
T = 512
D = 2048
HALF = 512
ALL = ("z", "y", "c", "x")
MESH = pl.DeviceIdType.MESH
F32 = jnp.float32
BF16 = jnp.bfloat16

fsq_levels = (8, 8, 8, 5, 5, 5)
fsq_bases = (1, 8, 64, 512, 2560, 12800)

NT = (((1,), (1,)), ((), ()))
TN = (((0,), (0,)), ((), ()))


def dot(a, b, dims=None):
    if dims is None:
        return jnp.dot(a, b, preferred_element_type=F32)
    return lax.dot_general(a, b, dims, preferred_element_type=F32)


def entry_barrier(devices):
    barrier = pltpu.get_barrier_semaphore()
    for device in devices:
        pl.semaphore_signal(barrier, inc=1, device_id=device, device_id_type=MESH)
    pl.semaphore_wait(barrier, len(devices))


def send(src, dst, ssem, rsem, device):
    copy = pltpu.make_async_remote_copy(
        src_ref=src, dst_ref=dst, send_sem=ssem, recv_sem=rsem, device_id=device, device_id_type=MESH
    )
    copy.start()
    return copy


def ring(axis, step):
    return lax.rem(lax.axis_index(axis) + step, 4)


def m1_kernel(
    numt_ref, proj_ref, resid_ref, og_ref, gain_ref, wq_hbm, wk_hbm, wv_hbm,
    xt_ref, g_ref, numt_all, gain_out,
    wbuf, wsem, xs, xr, xssem, xrsem, gs, gr, gssem, grsem, ns, nr, nssem, nrsem,
    xb, q, k, v, sq, sk, og, sc, att, datt, dk, dv,
    blk, pre, ssend, srecv, s2send, s2recv, sssem, srsem,
):
    c = lax.axis_index("c")
    peer = {"c": 1 - c}
    y = lax.axis_index("y")
    z = lax.axis_index("z")
    own_col = pl.multiple_of(c * HALF, HALF)
    peer_col = pl.multiple_of((1 - c) * HALF, HALF)

    loads = []
    for n, w in enumerate((wk_hbm, wv_hbm, wq_hbm)):
        cp = pltpu.make_async_copy(w.at[:, pl.ds(own_col, HALF)], wbuf.at[n], wsem.at[n])
        cp.start()
        loads.append(cp)
    entry_barrier([peer] + [{"y": ring("y", s)} for s in (1, 2, 3)] + [{"z": ring("z", s)} for s in (1, 2, 3)])

    copies = []
    for r in range(2):
        rows = pl.ds(r * 256, 256)
        add = dot(numt_ref[:, rows], proj_ref[...], TN)
        x = (resid_ref[rows, :].astype(F32) + add).astype(BF16)
        xb[0, rows, :] = x
        xs[rows, :] = x.astype(F32)
        copies.append(send(xs.at[rows], xr.at[rows], xssem.at[r], xrsem.at[r], peer))
    gs[...] = og_ref[:, pl.ds(peer_col, HALF)].astype(F32)
    copies.append(send(gs, gr, gssem, grsem, peer))
    ns[...] = numt_ref[0:16, :].astype(F32)
    copies.append(send(ns, nr, nssem, nrsem, peer))

    def project(slot, n, base):
        for half in range(2):
            p = dot(xb[slot], wbuf[n, :, half * 256 : half * 256 + 256])
            for hh in range(2):
                a = p[:, hh * DH : hh * DH + DH]
                at = base + half * 2 + hh
                if n == 1:
                    v[at] = a.astype(BF16)
                else:
                    s = 1.0 / (1.0 + jnp.exp(-a))
                    slope = s * (1.0 + a * (1.0 - s))
                    if n == 0:
                        k[at] = (a * s).astype(BF16)
                        sk[at] = slope
                    else:
                        q[at] = (a * s).astype(BF16)
                        sq[at] = slope

    mine = c * 4
    other = (1 - c) * 4
    for n in range(3):
        loads[n].wait()
        project(0, n, mine)
    for h in range(4):
        og[mine + h] = og_ref[:, pl.ds(pl.multiple_of(c * HALF + h * DH, DH), DH)]
    for r in range(2):
        copies[r].wait()
        xb[1, pl.ds(r * 256, 256), :] = xr[pl.ds(r * 256, 256), :].astype(BF16)
    project(1, 0, other)
    project(1, 1, other)

    def scan_start(s):
        ssend[s, 0] = blk[s, 0, 0:2] + blk[s, 1, 0:2]
        ssend[s, 1] = blk[s, 0, 2:4] + blk[s, 1, 2:4]
        out = []
        for half, axis in ((0, "y"), (1, "z")):
            for d in (1, 2, 3):
                out.append(send(ssend.at[s, half], srecv.at[s, half, d - 1], sssem.at[s, 0, half, d - 1],
                                srsem.at[s, 0, half, d - 1], {axis: ring(axis, d)}))
        return out

    def before(place, d, s):
        return (d <= place) if s == 0 else (d > place)

    def scan_middle(s, sent):
        for cp in sent:
            cp.wait()
        total = ssend[s, 0]
        inside = jnp.zeros_like(total)
        for d in (1, 2, 3):
            piece = srecv[s, 0, d - 1]
            total = total + piece
            inside = inside + jnp.where(before(y, d, s), piece, 0.0)
        s2send[s, 0] = total
        pre[s, 0:2] = inside
        passed = jnp.zeros_like(total)
        for d in (1, 2, 3):
            passed = passed + jnp.where(before(z, d, s), srecv[s, 1, d - 1], 0.0)
        s2send[s, 1] = passed
        s2send[s, 2] = passed + ssend[s, 1]
        pre[s, 2:4] = passed
        out = []
        for d in (1, 2, 3):
            out.append(send(s2send.at[s, 0], s2recv.at[s, 0, d - 1], sssem.at[s, 1, 0, d - 1],
                            srsem.at[s, 1, 0, d - 1], {"z": ring("z", d)}))
            wraps = (y + d) // 4
            pick = 2 - wraps if s == 0 else 1 + wraps
            out.append(send(s2send.at[s, pick], s2recv.at[s, 1, d - 1], sssem.at[s, 1, 1, d - 1],
                            srsem.at[s, 1, 1, d - 1], {"y": ring("y", d)}))
        return out

    def scan_end(s, sent):
        for cp in sent:
            cp.wait()
        first = pre[s, 0:2]
        second = pre[s, 2:4]
        for d in (1, 2, 3):
            first = first + jnp.where(before(z, d, s), s2recv[s, 0, d - 1], 0.0)
            second = second + s2recv[s, 1, d - 1]
        pre[s, 0:2] = first
        pre[s, 2:4] = second

    def state(s, b, h):
        base = pre[s, h]
        if s == 0:
            return (base + jnp.where(b == 1, blk[0, 0, h], 0.0)).astype(BF16)
        return (base + jnp.where(b == 0, blk[1, 1, h], 0.0)).astype(BF16)

    def kv_step(n, _):
        blk[0, n // 4, lax.rem(n, 4)] = dot(k[n], v[n], TN)
        return 0

    lax.fori_loop(0, 8, kv_step, 0)
    sent = scan_start(0)
    project(1, 2, other)
    copies[2].wait()
    for h in range(4):
        og[other + h] = gr[:, h * DH : h * DH + DH].astype(BF16)
    copies[3].wait()
    numt_all[c] = numt_ref[0:16, :]
    numt_all[1 - c] = nr[...].astype(BF16)
    sent = scan_middle(0, sent)

    row_ids = lax.broadcasted_iota(jnp.int32, (T, T), 0)
    col_ids = lax.broadcasted_iota(jnp.int32, (T, T), 1)

    def score_step(n, _):
        s = jnp.where(col_ids <= row_ids, dot(q[n], k[n], NT), 0.0).astype(BF16)
        sc[n] = s
        att[n] = dot(s, v[n])
        return 0

    lax.fori_loop(0, 8, score_step, 0)
    scan_end(0, sent)

    def forward_step(n, _):
        b = n // 4
        h = lax.rem(n, 4)
        a = att[n] + dot(q[n], state(0, b, h))
        root = jnp.sqrt(jnp.mean(a * a, axis=-1, keepdims=True) + 1e-06)
        inv = 1.0 / root
        normed = a * inv
        g = og[n].astype(F32)
        dn = g * gain_ref[h]
        da = ((dn - normed * jnp.mean(dn * normed, axis=-1, keepdims=True)) * inv).astype(BF16)
        datt[n] = da
        att[n, 0:1, :] = jnp.sum(g * normed, axis=0, keepdims=True)
        blk[1, b, h] = dot(q[n], da, TN)
        return 0

    lax.fori_loop(0, 8, forward_step, 0)
    sent = scan_start(1)
    for h in range(4):
        gain_out[:, h * DH : h * DH + DH] = att[h, 0:1, :] + att[4 + h, 0:1, :]

    def put(kind, n, value):
        b = n // 4
        h = lax.rem(n, 4)
        g_ref[kind * 2 + h // 2, pl.ds(pl.multiple_of(b * T, T), T),
              pl.ds(pl.multiple_of(lax.rem(h, 2) * DH, DH), DH)] = value.astype(BF16)

    def back_step(n, _):
        b = n // 4
        h = lax.rem(n, 4)
        da = datt[n]
        bs = jnp.where(col_ids <= row_ids, dot(da, v[n], NT), 0.0).astype(BF16)
        dq = dot(bs, k[n]) + dot(da, state(0, b, h), NT)
        put(0, n, dq * sq[n])
        dk[n] = dot(bs, q[n], TN)
        dv[n] = dot(sc[n], da, TN)
        return 0

    lax.fori_loop(0, 4, back_step, 0)
    sent = scan_middle(1, sent)
    lax.fori_loop(4, 8, back_step, 0)

    def turn_step(n, _):
        cols = pl.ds(pl.multiple_of(n * 128, 128), 128)
        for slot in range(2):
            place = c if slot == 0 else 1 - c
            t = xb[slot, :, cols].T
            xt_ref[n // 4, lax.rem(n, 4), :, :, :, pl.ds(pl.multiple_of(place * T, T), T)] = t.reshape(2, 4, 16, T)
        return 0

    lax.fori_loop(0, 16, turn_step, 0)
    scan_end(1, sent)

    def last_step(n, _):
        st = state(1, n // 4, lax.rem(n, 4))
        put(1, n, (dk[n] + dot(v[n], st, NT)) * sk[n])
        put(2, n, dv[n] + dot(k[n], st))
        return 0

    lax.fori_loop(0, 8, last_step, 0)


PLAN = (("x", 1), ("x", -1), ("y", 1), ("z", 1), ("y", -1), ("z", -1))
ORDER = {"x": ("x", "z", "y"), "y": ("y", "x", "z"), "z": ("z", "y", "x")}
DIMS = {"x": (4, 4, 2), "y": (4, 2, 4), "z": (4, 2, 4)}
DIMS2 = {"x": (4, 2), "y": (4, 2), "z": (2, 4)}


def m2_kernel(
    scale, xt_ref, g_ref, numt_ref, gain_ref, lev_ref, wq_hbm, wk_hbm, wv_hbm,
    wout, rg_out, gain_out, code_out, *scr,
):
    wbuf, wsem, igs, igr, igo, igsem, ar, arr, arsem, fs, fr, fsem, ps, pr, psem, sems = scr[:16]
    tx, t2 = scr[16:22], scr[22:28]
    recv = [[scr[28 + 18 * phase + 6 * m : 34 + 18 * phase + 6 * m] for m in range(3)] for phase in range(3)]
    c = lax.axis_index("c")
    peer = {"c": 1 - c}
    own_col = pl.multiple_of(c * HALF, HALF)
    peer_col = pl.multiple_of((1 - c) * HALF, HALF)
    loads = []
    for n, w in enumerate((wq_hbm, wk_hbm, wv_hbm)):
        cp = pltpu.make_async_copy(w.at[:, pl.ds(own_col, HALF)], wbuf.at[n], wsem.at[n])
        cp.start()
        loads.append(cp)
    entry_barrier([peer] + [{a: ring(a, s)} for a in ("x", "y", "z") for s in (1, 3)])

    def lhs(axis, i):
        if axis == "x":
            rows = xt_ref[:, :, :, i]
        elif axis == "y":
            rows = xt_ref[:, i]
        else:
            rows = xt_ref[i]
        return rows.reshape(512, 1024)

    def product(hp, i):
        axis = PLAN[hp][0]
        return dot(lhs(axis, i), g_ref[hp]).reshape(*DIMS[axis], 16, 256)

    sends = {}

    def go(hp, phase, m, src, dirn):
        axis = ORDER[PLAN[hp][0]][phase]
        sends[hp, phase, m] = send(src, recv[phase][m][hp], sems.at[0, hp, phase, m], sems.at[1, hp, phase, m],
                                   {axis: ring(axis, 1 if dirn == 1 else 3)})

    order = (2, 3, 0, 4, 5, 1)
    for hp in order:
        axis, d = PLAN[hp]
        tx[hp][0] = product(hp, ring(axis, 2))
        go(hp, 0, 0, tx[hp].at[0], d)
    for hp in order:
        axis, d = PLAN[hp]
        tx[hp][1] = product(hp, ring(axis, 3 if d == 1 else 1))
        go(hp, 0, 1, tx[hp].at[1], -d)
    for cp in loads:
        cp.wait()

    def ig_step(n, target, base):
        rows = pl.ds(pl.multiple_of(base + n * 128, 128), 128)
        total = None
        for t in range(3):
            left = jnp.concatenate([g_ref[2 * t, rows, :], g_ref[2 * t + 1, rows, :]], axis=1)
            part = dot(left, wbuf[t], NT)
            total = part if total is None else total + part
        target[pl.ds(pl.multiple_of(n * 128, 128), 128), :] = total
        return 0

    for hp in order:
        axis, d = PLAN[hp]
        mid = product(hp, ring(axis, 1 if d == 1 else 3))
        sends[hp, 0, 0].wait_recv()
        recv[0][0][hp][...] = recv[0][0][hp][...] + mid
        go(hp, 0, 2, recv[0][0][hp], d)
    for hp in range(6):
        s = dot(numt_ref[0], g_ref[hp, 0:T, :]) + dot(numt_ref[1], g_ref[hp, T : 2 * T, :])
        ar[0, hp] = s[0:8]
    for hp in range(2):
        ar[0, hp, 6:7, :] = gain_ref[:, hp * 256 : hp * 256 + 256]
    steps = [(a, m) for a in ("x", "y", "z") for m in (0, 1)]

    def small(n):
        axis, m = steps[n]
        i = lax.axis_index(axis)
        partner = 3 - i if m else i + 1 - 2 * lax.rem(i, 2)
        return send(ar.at[n], arr.at[n], arsem.at[0, n], arsem.at[1, n], {axis: partner})

    small_copy = small(0)
    lax.fori_loop(0, 4, lambda n, _: ig_step(n, igs, (1 - c) * T), 0)
    ig_copy = send(igs, igr, igsem.at[0], igsem.at[1], peer)
    for hp in order:
        tx[hp][2] = product(hp, ring(PLAN[hp][0], 0))

    def small_next(n, cp):
        cp.wait()
        ar[n + 1] = ar[n] + arr[n]
        return small(n + 1) if n + 1 < 6 else None

    small_copy = small_next(0, small_copy)
    lax.fori_loop(0, 4, lambda n, _: ig_step(n, igo, c * T), 0)
    small_copy = small_next(1, small_copy)
    ig_copy.wait()
    rg_out[...] = (igo[...] + igr[...]).astype(BF16)
    for n in range(2, 6):
        small_copy = small_next(n, small_copy)

    code = jnp.zeros((8, D), F32)
    for hp in range(6):
        s = ar[6, hp]
        if hp < 2:
            ps[:, D + hp * 256 : D + hp * 256 + 256] = s
        s = s * lev_ref[...]
        for _ in range(3):
            part = s.astype(BF16)
            s = s - part.astype(F32)
            code = code + dot(part, wbuf[hp // 2, :, (hp % 2) * 256 : (hp % 2) * 256 + 256], NT)
    ps[:, 0:D] = code
    p_copy = send(ps, pr, psem.at[0], psem.at[1], peer)

    def piece(hp, phase, i):
        axis = PLAN[hp][0]
        if phase == 1:
            return tx[hp].at[2, :, :, i] if axis == "y" else tx[hp].at[2, i]
        return t2[hp].at[:, i] if axis == "z" else t2[hp].at[i]

    for phase in (1, 2):
        for hp in order:
            axis, d = ORDER[PLAN[hp][0]][phase], PLAN[hp][1]
            sends[hp, phase - 1, 1].wait_recv()
            sends[hp, phase - 1, 2].wait_recv()
            arrived = recv[phase - 1][1][hp][...] + recv[phase - 1][2][hp][...]
            if phase == 1:
                tx[hp][2] = tx[hp][2] + arrived
            else:
                t2[hp][...] = piece(hp, 1, ring(ORDER[PLAN[hp][0]][1], 0))[...] + arrived
            go(hp, phase, 0, piece(hp, phase, ring(axis, 2)), d)
            go(hp, phase, 1, piece(hp, phase, ring(axis, 3 if d == 1 else 1)), -d)
        for hp in order:
            axis, d = ORDER[PLAN[hp][0]][phase], PLAN[hp][1]
            sends[hp, phase, 0].wait_recv()
            relay = recv[phase][0][hp]
            relay[...] = relay[...] + piece(hp, phase, ring(axis, 1 if d == 1 else 3))[...]
            go(hp, phase, 2, relay, d)

    for hp in range(6):
        sends[hp, 2, 1].wait_recv()
        sends[hp, 2, 2].wait_recv()
        last = ORDER[PLAN[hp][0]][2]
        fs[:, :, hp * 256 : hp * 256 + 256] = (
            piece(hp, 2, ring(last, 0))[...] + recv[2][1][hp][...] + recv[2][2][hp][...]
        ) * scale
    f_copy = send(fs.at[1 - c], fr, fsem.at[0], fsem.at[1], peer)
    for t in range(3):
        wout[t, :, pl.ds(own_col, HALF)] = fs[c, :, t * HALF : t * HALF + HALF]
    p_copy.wait()
    code_out[...] = (ps[:, 0:D] + pr[:, 0:D]) * scale
    gain_out[:, pl.ds(own_col, HALF)] = ps[:, D:] * scale
    gain_out[:, pl.ds(peer_col, HALF)] = pr[:, D:] * scale
    f_copy.wait()
    for t in range(3):
        wout[t, :, pl.ds(peer_col, HALF)] = fr[:, t * HALF : t * HALF + HALF]
    for cp in sends.values():
        cp.wait_send()


def vmem(*shape, dtype=F32):
    return pltpu.VMEM(shape, dtype)


def body(resid, token_ids, code_proj, w_query, w_key, w_value, gain, out_grad):
    dma = pltpu.SemaphoreType.DMA
    levels = jnp.array(fsq_levels, jnp.int32)[:, None]
    bases = jnp.array(fsq_bases, jnp.int32)[:, None]
    nums = (2 * (token_ids // bases % levels) - (levels - 1)).astype(BF16)
    nums = jnp.pad(nums, ((0, 10), (0, 0)))
    inv = 1.0 / (jnp.array(fsq_levels, F32) - 1.0)[:, None]
    rest = code_proj * inv
    terms = []
    for _ in range(3):
        term = lax.reduce_precision(rest, 8, 7)
        terms.append(jnp.pad(term.astype(BF16), ((0, 10), (0, 0))))
        rest = rest - term
    proj3 = jnp.concatenate(terms, axis=0)
    numt = jnp.concatenate([nums, nums, nums], axis=0)
    c = lax.axis_index("c")
    gain_heads = lax.dynamic_slice(gain, (c * HALF,), (HALF,)).reshape(4, 1, DH)
    any_spec = pl.BlockSpec(memory_space=pl.ANY)
    vm = pl.BlockSpec(memory_space=pltpu.VMEM)
    sds = jax.ShapeDtypeStruct
    xt, g, numt_all, gain_row = pl.pallas_call(
        m1_kernel,
        name="m1",
        out_shape=(sds((4, 4, 2, 4, 16, 2 * T), BF16), sds((6, 2 * T, 256), BF16), sds((2, 16, T), BF16), sds((1, HALF), F32)),
        in_specs=[vm] * 5 + [any_spec] * 3,
        out_specs=(vm,) * 4,
        scratch_shapes=[
            vmem(3, D, HALF, dtype=BF16), dma((3,)),
            vmem(T, D), vmem(T, D), dma((2,)), dma((2,)),
            vmem(T, HALF), vmem(T, HALF), dma, dma,
            vmem(16, T), vmem(16, T), dma, dma,
            vmem(2, T, D, dtype=BF16),
            vmem(8, T, DH, dtype=BF16), vmem(8, T, DH, dtype=BF16), vmem(8, T, DH, dtype=BF16),
            vmem(8, T, DH), vmem(8, T, DH), vmem(8, T, DH, dtype=BF16), vmem(8, T, T, dtype=BF16),
            vmem(8, T, DH), vmem(8, T, DH, dtype=BF16), vmem(8, T, DH), vmem(8, T, DH),
            vmem(2, 2, 4, DH, DH), vmem(2, 4, DH, DH),
            vmem(2, 2, 2, DH, DH), vmem(2, 2, 3, 2, DH, DH), vmem(2, 3, 2, DH, DH), vmem(2, 2, 3, 2, DH, DH),
            dma((2, 2, 2, 3)), dma((2, 2, 2, 3)),
        ],
        compiler_params=pltpu.CompilerParams(collective_id=0, has_side_effects=True, vmem_limit_bytes=VMEM_LIMIT),
    )(numt, proj3, resid[0], out_grad[0], gain_heads, w_query, w_key, w_value)

    scale = 1.0 / math.sqrt(T * lax.axis_size(ALL))
    lev = jnp.pad(inv, ((0, 2), (0, 0)))
    lev = jnp.broadcast_to(lev, (8, 256))
    w_out, resid_grad, gain_out, code_out = pl.pallas_call(
        functools.partial(m2_kernel, scale),
        name="m2",
        out_shape=(sds((3, 16, 2 * HALF), F32), sds((T, D), BF16), sds((8, 2 * HALF), F32), sds((8, D), F32)),
        in_specs=[vm] * 5 + [any_spec] * 3,
        out_specs=(vm,) * 4,
        scratch_shapes=[
            vmem(3, D, HALF, dtype=BF16), dma((3,)),
            vmem(T, D), vmem(T, D), vmem(T, D), dma((2,)),
            vmem(7, 6, 8, 256), vmem(6, 6, 8, 256), dma((2, 6)),
            vmem(2, 16, 3 * HALF), vmem(16, 3 * HALF), dma((2,)),
            vmem(8, D + HALF), vmem(8, D + HALF), dma((2,)),
            dma((2, 6, 3, 3)),
            *[vmem(3, *DIMS[a], 16, 256) for a, _ in PLAN],
            *[vmem(*DIMS2[a], 16, 256) for a, _ in PLAN],
            *[vmem(*DIMS[a], 16, 256) for _ in range(3) for a, _ in PLAN],
            *[vmem(*DIMS2[a], 16, 256) for _ in range(3) for a, _ in PLAN],
            *[vmem(2, 16, 256) for _ in range(3) for a, _ in PLAN],
        ],
        compiler_params=pltpu.CompilerParams(collective_id=1, has_side_effects=True, vmem_limit_bytes=VMEM_LIMIT),
    )(xt, g, numt_all, gain_row, lev, w_query, w_key, w_value)
    return resid_grad[None], w_out.transpose(1, 0, 2), gain_out[6], code_out[0:6]


VMEM_LIMIT = 66_000_000


def solution(mesh):
    finer = Mesh(mesh.devices.reshape(4, 4, 2, 4), ALL)
    seq = ("z", "y", "c")
    return jax.shard_map(
        body,
        mesh=finer,
        in_specs=(P("x", seq, None), P("x", seq), P(), P(), P(), P(), P(), P("x", seq, None)),
        out_specs=(P("x", seq, None), P(ALL, None, None), P(), P()),
        check_vma=False,
    )
```

```python
import functools
import math

import jax
import jax.numpy as jnp
from jax import lax
from jax.experimental import pallas as pl
from jax.experimental.pallas import tpu as pltpu
from jax.sharding import Mesh
from jax.sharding import PartitionSpec as P

HEADS = 8
DH = 128
T = 512
D = 2048
HALF = 512
ALL = ("z", "y", "c", "x")
MESH = pl.DeviceIdType.MESH
F32 = jnp.float32
BF16 = jnp.bfloat16

fsq_levels = (8, 8, 8, 5, 5, 5)
fsq_bases = (1, 8, 64, 512, 2560, 12800)

NT = (((1,), (1,)), ((), ()))
TN = (((0,), (0,)), ((), ()))


def dot(a, b, dims=None):
    if dims is None:
        return jnp.dot(a, b, preferred_element_type=F32)
    return lax.dot_general(a, b, dims, preferred_element_type=F32)


def entry_barrier(devices):
    barrier = pltpu.get_barrier_semaphore()
    for device in devices:
        pl.semaphore_signal(barrier, inc=1, device_id=device, device_id_type=MESH)
    pl.semaphore_wait(barrier, len(devices))


def send(src, dst, ssem, rsem, device):
    copy = pltpu.make_async_remote_copy(
        src_ref=src, dst_ref=dst, send_sem=ssem, recv_sem=rsem, device_id=device, device_id_type=MESH
    )
    copy.start()
    return copy


def ring(axis, step):
    return lax.rem(lax.axis_index(axis) + step, 4)


PLAN = (("x", 1), ("x", -1), ("y", 1), ("z", 1), ("y", -1), ("z", -1))
ORDER = {"x": ("x", "z", "y"), "y": ("y", "x", "z"), "z": ("z", "y", "x")}
DIMS = {"x": (4, 4, 2), "y": (4, 2, 4), "z": (4, 2, 4)}
DIMS2 = {"x": (4, 2), "y": (4, 2), "z": (2, 4)}


class Trace:
    on = False
    scope = None

    def __call__(self, name=None):
        if not self.on:
            return
        if self.scope is not None:
            self.scope.__exit__(None, None, None)
        self.scope = jax.named_scope(name) if name else None
        if name:
            self.scope.__enter__()


def kernel(
    scale, ids_ref, proj_ref, gain_ref, resid_hbm, og_hbm, wq_hbm, wk_hbm, wv_hbm,
    wout, rg_hbm, gain_out, code_out,
    wbuf, wsem, xb, q, k, v, sqk, dkv, og, ogsem, sc, datt, nf, ns, nall, proj3, gain_row,
    xssem, xrsem, gsem, nsem, free_sem,
    blk, pre, ssend, srecv, s2send, s2recv, sssem, srsem,
    xt_ref, g_ref, igsem, ar, arr, arsem, fs, fr, fsem, rgsem, sems, *scr,
):
    tr = Trace()
    tx, t2 = scr[0:6], scr[6:12]
    recv = [[scr[12 + 18 * phase + 6 * m : 18 + 18 * phase + 6 * m] for m in range(3)] for phase in range(3)]
    c = lax.axis_index("c")
    peer = {"c": 1 - c}
    y = lax.axis_index("y")
    z = lax.axis_index("z")
    own_col = pl.multiple_of(c * HALF, HALF)
    peer_col = pl.multiple_of((1 - c) * HALF, HALF)
    mine = c * 4
    other = (1 - c) * 4

    tr("enter")
    xload = pltpu.make_async_copy(resid_hbm, xb.at[0], ogsem.at[8])
    xload.start()
    loads = []
    for n, w in enumerate((wk_hbm, wv_hbm, wq_hbm)):
        cp = pltpu.make_async_copy(w.at[:, pl.ds(own_col, HALF)], wbuf.at[n], wsem.at[n])
        cp.start()
        loads.append(cp)
    ogloads = []
    for h in range(4):
        for m, (first, col) in enumerate(((other, peer_col), (mine, own_col))):
            cp = pltpu.make_async_copy(
                og_hbm.at[:, pl.ds(pl.multiple_of(col + h * DH, DH), DH)], og.at[first + h], ogsem.at[m * 4 + h])
            cp.start()
            ogloads.append(cp)

    ids = ids_ref[...].astype(F32)
    nf[...] = jnp.zeros_like(nf)
    rest = jnp.zeros((8, D), F32)
    row = lax.broadcasted_iota(jnp.int32, (8, 1), 0)
    inv_level = jnp.zeros((8, 1), F32)
    for j, (level, base) in enumerate(zip(fsq_levels, fsq_bases)):
        quot = jnp.floor((ids + 0.5) * (1.0 / base)) if base > 1 else ids
        digit = quot - level * jnp.floor((quot + 0.5) * (1.0 / level))
        nf[j : j + 1, :] = 2.0 * digit - (level - 1.0)
        inv_level = jnp.where(row == j, 1.0 / (level - 1.0), inv_level)
    proj3[...] = jnp.zeros_like(proj3)
    rest = proj_ref[...] * inv_level[0:6]
    for t in range(3):
        term = rest.astype(BF16)
        proj3[t, 0:6, :] = term
        rest = rest - term.astype(F32)
    nums = nf[...].astype(BF16)
    numt = jnp.concatenate([nums, nums, nums], axis=0)

    barrier_set = [peer] + [{"y": ring("y", s)} for s in (1, 2, 3)] + [{"z": ring("z", s)} for s in (1, 2, 3)]
    entry_barrier(barrier_set + [{"x": ring("x", s)} for s in (1, 3)])

    tr("inputs")
    xload.wait()
    xcopies = []
    for j in range(8):
        cols = slice(j * 256, j * 256 + 256)
        add = dot(numt, proj3[:, :, cols].reshape(48, 256), TN)
        x = (xb[0, :, cols].astype(F32) + add).astype(BF16)
        xb[0, :, cols] = x
        src, dst = tx[2 + j % 4].at[j // 4], recv[0][1 + j // 4][2 + j % 4]
        src[...] = x.astype(F32).reshape(4, 2, 4, 16, 256)
        xcopies.append(send(src, dst, xssem.at[j], xrsem.at[j], peer))
    for h in range(4):
        ogloads[2 * h].wait()
        dkv[h] = og[other + h].astype(F32)
    g_copy = send(dkv.at[0:4], dkv.at[4:8], gsem.at[0], gsem.at[1], peer)
    n_copy = send(nf, ns, nsem.at[0], nsem.at[1], peer)

    def project(slot, n, base):
        for half in range(2):
            p = dot(xb[slot], wbuf[n, :, half * 256 : half * 256 + 256])
            for hh in range(2):
                a = p[:, hh * DH : hh * DH + DH]
                at = base + half * 2 + hh
                if n == 1:
                    v[at] = a.astype(BF16)
                else:
                    s = 1.0 / (1.0 + jnp.exp(-a))
                    slope = s * (1.0 + a * (1.0 - s))
                    if n == 0:
                        k[at] = (a * s).astype(BF16)
                        sqk[8 + at] = slope
                    else:
                        q[at] = (a * s).astype(BF16)
                        sqk[at] = slope

    tr("own_proj")
    for n in range(3):
        loads[n].wait()
        project(0, n, mine)
    for h in range(4):
        ogloads[2 * h + 1].wait()
    tr("peer_wait")
    for j in range(8):
        xcopies[j].wait()
        xb[1, :, j * 256 : j * 256 + 256] = recv[0][1 + j // 4][2 + j % 4][...].reshape(512, 256).astype(BF16)
    tr("peer_kv")
    project(1, 0, other)
    project(1, 1, other)

    def scan_start(s):
        ssend[s, 0] = blk[s, 0, 0:2] + blk[s, 1, 0:2]
        ssend[s, 1] = blk[s, 0, 2:4] + blk[s, 1, 2:4]
        out = []
        for d in (2, 1, 3):
            for half, axis in ((0, "y"), (1, "z")):
                out.append(send(ssend.at[s, half], srecv.at[s, half, d - 1], sssem.at[s, 0, half, d - 1],
                                srsem.at[s, 0, half, d - 1], {axis: ring(axis, d)}))
        return out

    def before(place, d, s):
        return (d <= place) if s == 0 else (d > place)

    def scan_middle(s, sent):
        for cp in sent:
            cp.wait()
        total = ssend[s, 0]
        inside = jnp.zeros_like(total)
        passed = jnp.zeros_like(total)
        for d in (1, 2, 3):
            piece = srecv[s, 0, d - 1]
            total = total + piece
            inside = inside + jnp.where(before(y, d, s), piece, 0.0)
            passed = passed + jnp.where(before(z, d, s), srecv[s, 1, d - 1], 0.0)
        s2send[s, 0] = total
        pre[s, 0:2] = inside
        s2send[s, 1] = passed
        s2send[s, 2] = passed + ssend[s, 1]
        pre[s, 2:4] = passed
        out = []
        for d in (2, 1, 3):
            out.append(send(s2send.at[s, 0], s2recv.at[s, 0, d - 1], sssem.at[s, 1, 0, d - 1],
                            srsem.at[s, 1, 0, d - 1], {"z": ring("z", d)}))
            wraps = (y + d) // 4
            pick = 2 - wraps if s == 0 else 1 + wraps
            out.append(send(s2send.at[s, pick], s2recv.at[s, 1, d - 1], sssem.at[s, 1, 1, d - 1],
                            srsem.at[s, 1, 1, d - 1], {"y": ring("y", d)}))
        return out

    def scan_end(s, sent):
        for cp in sent:
            cp.wait()
        first = pre[s, 0:2]
        second = pre[s, 2:4]
        for d in (1, 2, 3):
            first = first + jnp.where(before(z, d, s), s2recv[s, 0, d - 1], 0.0)
            second = second + s2recv[s, 1, d - 1]
        pre[s, 0:2] = first
        pre[s, 2:4] = second

    def state(s, b, h):
        base = pre[s, h]
        if s == 0:
            return (base + jnp.where(b == 1, blk[0, 0, h], 0.0)).astype(BF16)
        return (base + jnp.where(b == 0, blk[1, 1, h], 0.0)).astype(BF16)

    def kv_step(n, _):
        blk[0, n // 4, lax.rem(n, 4)] = dot(k[n], v[n], TN)
        return 0

    tr("kv")
    lax.fori_loop(0, 8, kv_step, 0)
    sent = scan_start(0)
    tr("qpeer")
    project(1, 2, other)
    g_copy.wait()
    for h in range(4):
        og[other + h] = dkv[4 + h].astype(BF16)
    n_copy.wait()
    nall[c] = nums
    nall[1 - c] = ns[...].astype(BF16)

    row_ids = lax.broadcasted_iota(jnp.int32, (T, T), 0)
    col_ids = lax.broadcasted_iota(jnp.int32, (T, T), 1)

    def score_step(n, _):
        s = jnp.where(col_ids <= row_ids, dot(q[n], k[n], NT), 0.0).astype(BF16)
        sc[n] = s
        dkv[8 + n] = dot(s, v[n])
        return 0

    tr("scores1")
    lax.fori_loop(0, 5, score_step, 0)
    tr("scanmid0")
    sent = scan_middle(0, sent)
    tr("scores2")
    lax.fori_loop(5, 8, score_step, 0)

    def turn_step(n, _):
        cols = pl.ds(pl.multiple_of(n * 128, 128), 128)
        for slot in range(2):
            place = c if slot == 0 else 1 - c
            t = xb[slot, :, cols].T
            xt_ref[n // 4, lax.rem(n, 4), :, :, :, pl.ds(pl.multiple_of(place * T, T), T)] = t.reshape(2, 4, 16, T)
        return 0

    tr("turn")
    lax.fori_loop(0, 16, turn_step, 0)
    tr("scanend0")
    scan_end(0, sent)

    def forward_step(n, _):
        b = n // 4
        h = lax.rem(n, 4)
        a = dkv[8 + n] + dot(q[n], state(0, b, h))
        root = jnp.sqrt(jnp.mean(a * a, axis=-1, keepdims=True) + 1e-06)
        inv = 1.0 / root
        normed = a * inv
        g = og[n].astype(F32)
        dn = g * gain_ref[:, pl.ds(pl.multiple_of(c * HALF + h * DH, DH), DH)]
        da = ((dn - normed * jnp.mean(dn * normed, axis=-1, keepdims=True)) * inv).astype(BF16)
        datt[n] = da
        gain_row[n] = jnp.sum(g * normed, axis=0, keepdims=True)
        blk[1, b, h] = dot(q[n], da, TN)
        return 0

    tr("fwd")
    lax.fori_loop(0, 8, forward_step, 0)
    sent = scan_start(1)

    def put(kind, n, value):
        b = n // 4
        h = lax.rem(n, 4)
        g_ref[kind * 2 + h // 2, pl.ds(pl.multiple_of(b * T, T), T),
              pl.ds(pl.multiple_of(lax.rem(h, 2) * DH, DH), DH)] = value.astype(BF16)

    def back_step(n, _):
        b = n // 4
        h = lax.rem(n, 4)
        da = datt[n]
        bs = jnp.where(col_ids <= row_ids, dot(da, v[n], NT), 0.0).astype(BF16)
        dq = dot(bs, k[n]) + dot(da, state(0, b, h), NT)
        put(0, n, dq * sqk[n])
        dkv[n] = dot(bs, q[n], TN)
        dkv[8 + n] = dot(sc[n], da, TN)
        return 0

    def lhs(axis, i):
        if axis == "x":
            rows = xt_ref[:, :, :, i]
        elif axis == "y":
            rows = xt_ref[:, i]
        else:
            rows = xt_ref[i]
        return rows.reshape(512, 1024)

    def product(hp, i):
        axis = PLAN[hp][0]
        return dot(lhs(axis, i), g_ref[hp]).reshape(*DIMS[axis], 16, 256)

    sends = {}

    def go(hp, phase, m, src, dirn):
        axis = ORDER[PLAN[hp][0]][phase]
        sends[hp, phase, m] = send(src, recv[phase][m][hp], sems.at[0, hp, phase, m], sems.at[1, hp, phase, m],
                                   {axis: ring(axis, 1 if dirn == 1 else 3)})

    def far(hps):
        for hp in hps:
            tx[hp][0] = product(hp, ring(PLAN[hp][0], 2))
        for hp in hps:
            go(hp, 0, 0, tx[hp].at[0], PLAN[hp][1])

    def straight(hps):
        for hp in hps:
            axis, d = PLAN[hp]
            tx[hp][1] = product(hp, ring(axis, 3 if d == 1 else 1))
        for hp in hps:
            go(hp, 0, 1, tx[hp].at[1], -PLAN[hp][1])

    tr("back1")
    lax.fori_loop(0, 5, back_step, 0)
    tr("scanmid1")
    sent = scan_middle(1, sent)
    tr("back2")
    lax.fori_loop(5, 8, back_step, 0)
    tr("xfirst")
    far((0, 1))
    straight((0, 1))
    tr("scanend1")
    scan_end(1, sent)

    def last_step(n, _):
        st = state(1, n // 4, lax.rem(n, 4))
        put(1, n, (dkv[n] + dot(v[n], st, NT)) * sqk[8 + n])
        put(2, n, dkv[8 + n] + dot(k[n], st))
        return 0

    tr("last")
    lax.fori_loop(0, 8, last_step, 0)
    pl.semaphore_signal(free_sem, inc=1, device_id=peer, device_id_type=MESH)
    tr("yzfirst")
    far((2, 3))
    far((4, 5))
    straight((2, 3, 4, 5))

    tr("small")
    smalls = []
    for t in range(3):
        parts = []
        for hp in (2 * t, 2 * t + 1):
            s = dot(nall[0], g_ref[hp, 0:T, :]) + dot(nall[1], g_ref[hp, T : 2 * T, :])
            s = s[0:8] * inv_level
            terms = []
            for _ in range(3):
                term = s.astype(BF16).astype(F32)
                s = s - term
                terms.append(term)
            terms.append(jnp.zeros_like(s))
            parts.append(jnp.concatenate(terms, axis=0))
        smalls.append(jnp.concatenate(parts, axis=1).astype(BF16))

    order_w = (2, 0, 1)

    def ig_tile(n, base, extra):
        total = None
        rows = pl.ds(pl.multiple_of(base, T), T)
        for t in range(3):
            left = jnp.concatenate([g_ref[2 * t, rows, :], g_ref[2 * t + 1, rows, :]], axis=1)
            if extra:
                left = jnp.concatenate([left, smalls[t]], axis=0)
            part = dot(left, wbuf[order_w[t], pl.ds(pl.multiple_of(n * 256, 256), 256), :], NT)
            total = part if total is None else total + part
        return total

    def ig_peer(n, _):
        total = ig_tile(n, (1 - c) * T, True)
        dkv[2 * n] = total[0:T, 0:DH]
        dkv[2 * n + 1] = total[0:T, DH : 2 * DH]
        code = total[T : T + 8] + total[T + 8 : T + 16] + total[T + 16 : T + 24]
        ar[0, :, pl.ds(pl.multiple_of(n * 256, 256), 256)] = code
        return 0

    tr("ig1")
    lax.fori_loop(0, 8, ig_peer, 0)
    ar[0, 6:7, :] = jnp.zeros((1, D), F32)
    for h in range(4):
        ar[0, 6:7, pl.ds(pl.multiple_of(c * HALF + h * DH, DH), DH)] = gain_row[h] + gain_row[4 + h]

    steps = [("c", 0)] + [(a, m) for a in ("x", "y", "z") for m in (0, 1)]

    def small(n):
        axis, m = steps[n]
        i = lax.axis_index(axis)
        partner = 3 - i if m else i + 1 - 2 * lax.rem(i, 2)
        return send(ar.at[n], arr.at[n], arsem.at[0, n], arsem.at[1, n], {axis: partner})

    def small_next(n, cp):
        cp.wait()
        ar[n + 1] = ar[n] + arr[n]
        return small(n + 1) if n + 1 < 7 else None

    small_copy = small(0)
    pl.semaphore_wait(free_sem, 1)
    ig_copy = send(dkv, sqk, igsem.at[0], igsem.at[1], peer)

    def relay(hp):
        axis, d = PLAN[hp]
        mid = product(hp, ring(axis, 1 if d == 1 else 3))
        sends[hp, 0, 0].wait_recv()
        recv[0][0][hp][...] = recv[0][0][hp][...] + mid
        go(hp, 0, 2, recv[0][0][hp], d)

    tr("relay")
    small_copy = small_next(0, small_copy)
    for hp in (0, 1, 2, 3, 4, 5):
        relay(hp)
    tr("own")
    for hp in range(6):
        sends[hp, 0, 0].wait_send()
    for hp in range(6):
        tx[hp][0] = product(hp, ring(PLAN[hp][0], 0))

    tr("ig2")
    ig_copy.wait()

    def ig_own(n, _):
        total = ig_tile(n, c * T, False)
        total = total + jnp.concatenate([sqk[2 * n], sqk[2 * n + 1]], axis=1)
        xb[0, :, pl.ds(pl.multiple_of(n * 256, 256), 256)] = total.astype(BF16)
        return 0

    lax.fori_loop(0, 8, ig_own, 0)
    rg_copy = pltpu.make_async_copy(xb.at[0], rg_hbm, rgsem)
    rg_copy.start()

    def piece(hp, phase, i):
        axis = PLAN[hp][0]
        if phase == 1:
            return tx[hp].at[0, :, :, i] if axis == "y" else tx[hp].at[0, i]
        return t2[hp].at[:, i] if axis == "z" else t2[hp].at[i]

    order = (0, 1, 2, 3, 4, 5)
    stage = 1
    for phase in (1, 2):
        tr("ph%da" % phase)
        for hp in order:
            axis, d = ORDER[PLAN[hp][0]][phase], PLAN[hp][1]
            sends[hp, phase - 1, 1].wait_recv()
            sends[hp, phase - 1, 2].wait_recv()
            arrived = recv[phase - 1][1][hp][...] + recv[phase - 1][2][hp][...]
            if phase == 1:
                tx[hp][0] = tx[hp][0] + arrived
            else:
                t2[hp][...] = piece(hp, 1, ring(ORDER[PLAN[hp][0]][1], 0))[...] + arrived
            go(hp, phase, 0, piece(hp, phase, ring(axis, 2)), d)
            go(hp, phase, 1, piece(hp, phase, ring(axis, 3 if d == 1 else 1)), -d)
        small_copy = small_next(stage, small_copy)
        stage += 1
        tr("ph%db" % phase)
        for hp in order:
            axis, d = ORDER[PLAN[hp][0]][phase], PLAN[hp][1]
            sends[hp, phase, 0].wait_recv()
            via = recv[phase][0][hp]
            via[...] = via[...] + piece(hp, phase, ring(axis, 1 if d == 1 else 3))[...]
            go(hp, phase, 2, via, d)
        small_copy = small_next(stage, small_copy)
        stage += 1

    tr("final")
    for hp in range(6):
        sends[hp, 2, 1].wait_recv()
        sends[hp, 2, 2].wait_recv()
        last = ORDER[PLAN[hp][0]][2]
        fs[:, :, hp * 256 : hp * 256 + 256] = (
            piece(hp, 2, ring(last, 0))[...] + recv[2][1][hp][...] + recv[2][2][hp][...]
        ) * scale
    f_copy = send(fs.at[1 - c], fr, fsem.at[0], fsem.at[1], peer)
    for t in range(3):
        wout[t, :, pl.ds(own_col, HALF)] = fs[c, :, t * HALF : t * HALF + HALF]
    while stage < 7:
        small_copy = small_next(stage, small_copy)
        stage += 1
    code_out[...] = ar[7, 0:6, :] * scale
    gain_out[...] = ar[7, 6:7, 0 : 2 * HALF] * scale
    f_copy.wait()
    for t in range(3):
        wout[t, :, pl.ds(peer_col, HALF)] = fr[:, t * HALF : t * HALF + HALF]
    tr("drain")
    for (hp, phase, m), cp in sends.items():
        if (phase, m) != (0, 0):
            cp.wait_send()
    rg_copy.wait()
    tr()


def vmem(*shape, dtype=F32):
    return pltpu.VMEM(shape, dtype)


def body(resid, token_ids, code_proj, w_query, w_key, w_value, gain, out_grad):
    dma = pltpu.SemaphoreType.DMA
    any_spec = pl.BlockSpec(memory_space=pl.ANY)
    vm = pl.BlockSpec(memory_space=pltpu.VMEM)
    sds = jax.ShapeDtypeStruct
    scale = 1.0 / math.sqrt(T * lax.axis_size(ALL))
    w_out, resid_grad, gain_out, code_out = pl.pallas_call(
        functools.partial(kernel, scale),
        name="layer",
        out_shape=(sds((3, 16, 2 * HALF), F32), sds((T, D), BF16), sds((1, 2 * HALF), F32), sds((6, D), F32)),
        in_specs=[vm] * 3 + [any_spec] * 5,
        out_specs=(vm, any_spec, vm, vm),
        scratch_shapes=[
            vmem(3, D, HALF, dtype=BF16), dma((3,)), vmem(2, T, D, dtype=BF16),
            vmem(8, T, DH, dtype=BF16), vmem(8, T, DH, dtype=BF16), vmem(8, T, DH, dtype=BF16),
            vmem(16, T, DH), vmem(16, T, DH), vmem(8, T, DH, dtype=BF16), dma((9,)),
            vmem(8, T, T, dtype=BF16), vmem(8, T, DH, dtype=BF16),
            vmem(16, T), vmem(16, T), vmem(2, 16, T, dtype=BF16), vmem(3, 16, D, dtype=BF16), vmem(8, 1, DH),
            dma((8,)), dma((8,)), dma((2,)), dma((2,)), pltpu.SemaphoreType.REGULAR,
            vmem(2, 2, 4, DH, DH), vmem(2, 4, DH, DH),
            vmem(2, 2, 2, DH, DH), vmem(2, 2, 3, 2, DH, DH), vmem(2, 3, 2, DH, DH), vmem(2, 2, 3, 2, DH, DH),
            dma((2, 2, 2, 3)), dma((2, 2, 2, 3)),
            vmem(4, 4, 2, 4, 16, 2 * T, dtype=BF16), vmem(6, 2 * T, 256, dtype=BF16), dma((2,)),
            vmem(8, 8, D), vmem(7, 8, D), dma((2, 7)),
            vmem(2, 16, 3 * HALF), vmem(16, 3 * HALF), dma((2,)), dma,
            dma((2, 6, 3, 3)),
            *[vmem(2, *DIMS[a], 16, 256) for a, _ in PLAN],
            *[vmem(*DIMS2[a], 16, 256) for a, _ in PLAN],
            *[vmem(*DIMS[a], 16, 256) for _ in range(3) for a, _ in PLAN],
            *[vmem(*DIMS2[a], 16, 256) for _ in range(3) for a, _ in PLAN],
            *[vmem(2, 16, 256) for _ in range(3) for a, _ in PLAN],
        ],
        compiler_params=pltpu.CompilerParams(collective_id=0, has_side_effects=True, vmem_limit_bytes=67_043_328),
    )(token_ids, code_proj, gain[None], resid[0], out_grad[0], w_query, w_key, w_value)
    return resid_grad[None], w_out.transpose(1, 0, 2), gain_out[0], code_out


def solution(mesh):
    finer = Mesh(mesh.devices.reshape(4, 4, 2, 4), ALL)
    seq = ("z", "y", "c")
    return jax.shard_map(
        body,
        mesh=finer,
        in_specs=(P("x", seq, None), P("x", seq), P(), P(), P(), P(), P(), P("x", seq, None)),
        out_specs=(P("x", seq, None), P(ALL, None, None), P(), P()),
        check_vma=False,
    )
```

```python
import functools
import math

import jax
import jax.numpy as jnp
from jax import lax
from jax.experimental import pallas as pl
from jax.experimental.pallas import tpu as pltpu
from jax.sharding import Mesh
from jax.sharding import PartitionSpec as P

HEADS = 8
DH = 128
T = 512
D = 2048
HALF = 512
ALL = ("z", "y", "c", "x")
MESH = pl.DeviceIdType.MESH
F32 = jnp.float32
BF16 = jnp.bfloat16

fsq_levels = (8, 8, 8, 5, 5, 5)
fsq_bases = (1, 8, 64, 512, 2560, 12800)

NT = (((1,), (1,)), ((), ()))
TN = (((0,), (0,)), ((), ()))


def dot(a, b, dims=None):
    if dims is None:
        return jnp.dot(a, b, preferred_element_type=F32)
    return lax.dot_general(a, b, dims, preferred_element_type=F32)


def entry_barrier(devices):
    barrier = pltpu.get_barrier_semaphore()
    for device in devices:
        pl.semaphore_signal(barrier, inc=1, device_id=device, device_id_type=MESH)
    pl.semaphore_wait(barrier, len(devices))


def send(src, dst, ssem, rsem, device):
    copy = pltpu.make_async_remote_copy(
        src_ref=src, dst_ref=dst, send_sem=ssem, recv_sem=rsem, device_id=device, device_id_type=MESH
    )
    copy.start()
    return copy


def ring(axis, step):
    return lax.rem(lax.axis_index(axis) + step, 4)


PLAN = (("x", 1), ("x", -1), ("y", 1), ("z", 1), ("y", -1), ("z", -1))
ORDER = {"x": ("x", "z", "y"), "y": ("y", "x", "z"), "z": ("z", "y", "x")}
DIMS = {"x": (4, 4, 2), "y": (4, 2, 4), "z": (4, 2, 4)}
DIMS2 = {"x": (4, 2), "y": (4, 2), "z": (2, 4)}


class Trace:
    on = False
    scope = None

    def __call__(self, name=None):
        if not self.on:
            return
        if self.scope is not None:
            self.scope.__exit__(None, None, None)
        self.scope = jax.named_scope(name) if name else None
        if name:
            self.scope.__enter__()


def kernel(
    scale, ids_ref, proj_ref, gain_ref, resid_hbm, og_hbm, wq_hbm, wk_hbm, wv_hbm,
    wout, rg_hbm, gain_out, code_out,
    wbuf, wsem, xb, q, k, v, sqk, dkv, og, ogsem, sc, datt, nf, ns, nall, proj3, gain_row,
    xssem, xrsem, gsem, nsem, free_sem,
    blk, pre, sbuf, rbuf, obuf, sssem, srsem,
    xt_ref, g_ref, igsem, ar, arr, arsem, fs, fr, fsem, rgsem, sems, *scr,
):
    tr = Trace()

    def pairs(first, last, step):
        def two(i, _):
            step(2 * i)
            step(2 * i + 1)
            return 0

        lax.fori_loop(first // 2, last // 2, two, 0)

    tx, t2 = scr[0:6], scr[6:12]
    recv = [[scr[12 + 18 * phase + 6 * m : 18 + 18 * phase + 6 * m] for m in range(3)] for phase in range(3)]
    c = lax.axis_index("c")
    peer = {"c": 1 - c}
    y = lax.axis_index("y")
    z = lax.axis_index("z")
    own_col = pl.multiple_of(c * HALF, HALF)
    peer_col = pl.multiple_of((1 - c) * HALF, HALF)
    mine = c * 4
    other = (1 - c) * 4

    tr("enter")
    xload = pltpu.make_async_copy(resid_hbm, xb.at[0], ogsem.at[8])
    xload.start()
    loads = []
    for n, w in enumerate((wk_hbm, wv_hbm, wq_hbm)):
        cp = pltpu.make_async_copy(w.at[:, pl.ds(own_col, HALF)], wbuf.at[n], wsem.at[n])
        cp.start()
        loads.append(cp)
    ogloads = []
    for h in range(4):
        for m, (first, col) in enumerate(((other, peer_col), (mine, own_col))):
            cp = pltpu.make_async_copy(
                og_hbm.at[:, pl.ds(pl.multiple_of(col + h * DH, DH), DH)], og.at[first + h], ogsem.at[m * 4 + h])
            cp.start()
            ogloads.append(cp)

    ids = ids_ref[...].astype(F32)
    nf[...] = jnp.zeros_like(nf)
    rest = jnp.zeros((8, D), F32)
    row = lax.broadcasted_iota(jnp.int32, (8, 1), 0)
    inv_level = jnp.zeros((8, 1), F32)
    for j, (level, base) in enumerate(zip(fsq_levels, fsq_bases)):
        quot = jnp.floor((ids + 0.5) * (1.0 / base)) if base > 1 else ids
        digit = quot - level * jnp.floor((quot + 0.5) * (1.0 / level))
        nf[j : j + 1, :] = 2.0 * digit - (level - 1.0)
        inv_level = jnp.where(row == j, 1.0 / (level - 1.0), inv_level)
    proj3[...] = jnp.zeros_like(proj3)
    rest = proj_ref[...] * inv_level[0:6]
    for t in range(3):
        term = rest.astype(BF16)
        proj3[t, 0:6, :] = term
        rest = rest - term.astype(F32)
    nums = nf[...].astype(BF16)
    numt = jnp.concatenate([nums, nums, nums], axis=0)

    plane = [{"z": ring("z", dz), "y": ring("y", dy)} for dz in range(4) for dy in range(4) if dz or dy]
    entry_barrier([peer] + plane + [{"x": ring("x", n)} for n in (1, 2, 3)])

    tr("inputs")
    xload.wait()
    xcopies = []
    for j in range(8):
        cols = slice(j * 256, j * 256 + 256)
        add = dot(numt, proj3[:, :, cols].reshape(48, 256), TN)
        x = (xb[0, :, cols].astype(F32) + add).astype(BF16)
        xb[0, :, cols] = x
        src, dst = tx[2 + j % 4].at[j // 4], recv[0][1 + j // 4][2 + j % 4]
        src[...] = x.astype(F32).reshape(4, 2, 4, 16, 256)
        xcopies.append(send(src, dst, xssem.at[j], xrsem.at[j], peer))
    for h in range(4):
        ogloads[2 * h].wait()
        dkv[h] = og[other + h].astype(F32)
    g_copy = send(dkv.at[0:4], dkv.at[4:8], gsem.at[0], gsem.at[1], peer)
    n_copy = send(nf, ns, nsem.at[0], nsem.at[1], peer)

    def project(slot, n, base):
        for half in range(2):
            p = dot(xb[slot], wbuf[n, :, half * 256 : half * 256 + 256])
            for hh in range(2):
                a = p[:, hh * DH : hh * DH + DH]
                at = base + half * 2 + hh
                if n == 1:
                    v[at] = a.astype(BF16)
                else:
                    s = 1.0 / (1.0 + jnp.exp(-a))
                    slope = s * (1.0 + a * (1.0 - s))
                    if n == 0:
                        k[at] = (a * s).astype(BF16)
                        sqk[8 + at] = slope
                    else:
                        q[at] = (a * s).astype(BF16)
                        sqk[at] = slope

    def kv_step(n):
        blk[0, n // 4, lax.rem(n, 4)] = dot(k[n], v[n], TN)

    def kv_steps(base):
        for h in range(4):
            kv_step(base + h)

    tr("own_proj")
    for n in range(2):
        loads[n].wait()
        project(0, n, mine)
    kv_steps(mine)
    for h in range(4):
        ogloads[2 * h + 1].wait()
    tr("peer_wait")
    for j in range(8):
        xcopies[j].wait()
        xb[1, :, j * 256 : j * 256 + 256] = recv[0][1 + j // 4][2 + j % 4][...].reshape(512, 256).astype(BF16)
    tr("peer_kv")
    project(1, 0, other)
    project(1, 1, other)

    me = z * 4 + y
    spots = sorted(((dz, dy) for dz in range(4) for dy in range(4) if dz or dy),
                   key=lambda o: -(min(o[0], 4 - o[0]) + min(o[1], 4 - o[1])))

    def to_all(src, dst, n):
        out = []
        for o, (dz, dy) in enumerate(spots):
            zt, yt = ring("z", dz), ring("y", dy)
            out.append(send(src.at[zt * 4 + yt], dst.at[me], sssem.at[n, o], srsem.at[n, o], {"z": zt, "y": yt}))
        return out

    def scan_start(s):
        sbuf[s] = (blk[s, 0] + blk[s, 1]).reshape(16, 32, DH)
        out = to_all(sbuf.at[s], rbuf.at[s], 2 * s)
        rbuf[s, me] = sbuf[s, me]
        return out

    def scan_middle(s, sent):
        for cp in sent:
            cp.wait()
        total = jnp.zeros((32, DH), F32)
        for i in range(16) if s == 0 else reversed(range(16)):
            obuf[s, i] = total
            total = total + rbuf[s, i]
        out = to_all(obuf.at[s], pre.at[s], 2 * s + 1)
        pre[s, me] = obuf[s, me]
        return out

    def scan_end(s, sent):
        for cp in sent:
            cp.wait()

    def state(s, b, h):
        base = pre[s, pl.ds(4 * h, 4)].reshape(DH, DH)
        if s == 0:
            return (base + jnp.where(b == 1, blk[0, 0, h], 0.0)).astype(BF16)
        return (base + jnp.where(b == 0, blk[1, 1, h], 0.0)).astype(BF16)

    tr("kv")
    kv_steps(other)
    sent = scan_start(0)
    tr("qproj")
    loads[2].wait()
    project(0, 2, mine)
    project(1, 2, other)
    g_copy.wait()
    for h in range(4):
        og[other + h] = dkv[4 + h].astype(BF16)
    n_copy.wait()
    nall[c] = nums
    nall[1 - c] = ns[...].astype(BF16)

    row_ids = lax.broadcasted_iota(jnp.int32, (T, T), 0)
    col_ids = lax.broadcasted_iota(jnp.int32, (T, T), 1)

    def score_step(n):
        s = jnp.where(col_ids <= row_ids, dot(q[n], k[n], NT), 0.0).astype(BF16)
        sc[n] = s
        dkv[8 + n] = dot(s, v[n])

    tr("scores1")
    pairs(0, 4, score_step)
    tr("scanmid0")
    sent = scan_middle(0, sent)
    tr("scores2")
    pairs(4, 8, score_step)

    def turn_step(n):
        cols = pl.ds(pl.multiple_of(n * 128, 128), 128)
        for slot in range(2):
            place = c if slot == 0 else 1 - c
            t = xb[slot, :, cols].T
            xt_ref[n // 4, lax.rem(n, 4), :, :, :, pl.ds(pl.multiple_of(place * T, T), T)] = t.reshape(2, 4, 16, T)

    tr("turn")
    pairs(0, 16, turn_step)
    tr("scanend0")
    scan_end(0, sent)

    def forward_step(n):
        b = n // 4
        h = lax.rem(n, 4)
        a = dkv[8 + n] + dot(q[n], state(0, b, h))
        root = jnp.sqrt(jnp.mean(a * a, axis=-1, keepdims=True) + 1e-06)
        inv = 1.0 / root
        normed = a * inv
        g = og[n].astype(F32)
        dn = g * gain_ref[:, pl.ds(pl.multiple_of(c * HALF + h * DH, DH), DH)]
        da = ((dn - normed * jnp.mean(dn * normed, axis=-1, keepdims=True)) * inv).astype(BF16)
        datt[n] = da
        gain_row[n] = jnp.sum(g * normed, axis=0, keepdims=True)
        blk[1, b, h] = dot(q[n], da, TN)

    tr("fwd")
    pairs(0, 8, forward_step)
    sent = scan_start(1)

    def put(kind, n, value):
        b = n // 4
        h = lax.rem(n, 4)
        g_ref[kind * 2 + h // 2, pl.ds(pl.multiple_of(b * T, T), T),
              pl.ds(pl.multiple_of(lax.rem(h, 2) * DH, DH), DH)] = value.astype(BF16)

    def back_step(n):
        b = n // 4
        h = lax.rem(n, 4)
        da = datt[n]
        bs = jnp.where(col_ids <= row_ids, dot(da, v[n], NT), 0.0).astype(BF16)
        dq = dot(bs, k[n]) + dot(da, state(0, b, h), NT)
        put(0, n, dq * sqk[n])
        dkv[n] = dot(bs, q[n], TN)
        dkv[8 + n] = dot(sc[n], da, TN)

    def lhs(axis, i):
        if axis == "x":
            rows = xt_ref[:, :, :, i]
        elif axis == "y":
            rows = xt_ref[:, i]
        else:
            rows = xt_ref[i]
        return rows.reshape(512, 1024)

    def product(hp, i):
        axis = PLAN[hp][0]
        return dot(lhs(axis, i), g_ref[hp]).reshape(*DIMS[axis], 16, 256)

    sends = {}

    def go(hp, phase, m, src, dirn):
        axis = ORDER[PLAN[hp][0]][phase]
        sends[hp, phase, m] = send(src, recv[phase][m][hp], sems.at[0, hp, phase, m], sems.at[1, hp, phase, m],
                                   {axis: ring(axis, 1 if dirn == 1 else 3)})

    def far(hps):
        for hp in hps:
            tx[hp][0] = product(hp, ring(PLAN[hp][0], 2))
        for hp in hps:
            go(hp, 0, 0, tx[hp].at[0], PLAN[hp][1])

    def straight(hps):
        for hp in hps:
            axis, d = PLAN[hp]
            tx[hp][1] = product(hp, ring(axis, 3 if d == 1 else 1))
        for hp in hps:
            go(hp, 0, 1, tx[hp].at[1], -PLAN[hp][1])

    tr("back1")
    pairs(0, 4, back_step)
    tr("scanmid1")
    sent = scan_middle(1, sent)
    tr("back2")
    pairs(4, 8, back_step)
    tr("xfirst")
    far((0, 1))
    straight((0, 1))
    tr("scanend1")
    scan_end(1, sent)

    def last_step(n):
        st = state(1, n // 4, lax.rem(n, 4))
        put(1, n, (dkv[n] + dot(v[n], st, NT)) * sqk[8 + n])
        put(2, n, dkv[8 + n] + dot(k[n], st))

    tr("last")
    pairs(0, 8, last_step)
    pl.semaphore_signal(free_sem, inc=1, device_id=peer, device_id_type=MESH)
    tr("yzfirst")
    far((2, 3))
    far((4, 5))
    straight((2, 3, 4, 5))

    tr("small")
    smalls = []
    for t in range(3):
        parts = []
        for hp in (2 * t, 2 * t + 1):
            s = dot(nall[0], g_ref[hp, 0:T, :]) + dot(nall[1], g_ref[hp, T : 2 * T, :])
            s = s[0:8] * inv_level
            terms = []
            for _ in range(3):
                term = s.astype(BF16).astype(F32)
                s = s - term
                terms.append(term)
            terms.append(jnp.zeros_like(s))
            parts.append(jnp.concatenate(terms, axis=0))
        smalls.append(jnp.concatenate(parts, axis=1).astype(BF16))

    order_w = (2, 0, 1)

    def ig_tile(n, base, extra):
        total = None
        rows = pl.ds(pl.multiple_of(base, T), T)
        for t in range(3):
            left = jnp.concatenate([g_ref[2 * t, rows, :], g_ref[2 * t + 1, rows, :]], axis=1)
            if extra:
                left = jnp.concatenate([left, smalls[t]], axis=0)
            part = dot(left, wbuf[order_w[t], pl.ds(pl.multiple_of(n * 256, 256), 256), :], NT)
            total = part if total is None else total + part
        return total

    def ig_peer(n, _):
        total = ig_tile(n, (1 - c) * T, True)
        dkv[2 * n] = total[0:T, 0:DH]
        dkv[2 * n + 1] = total[0:T, DH : 2 * DH]
        code = total[T : T + 8] + total[T + 8 : T + 16] + total[T + 16 : T + 24]
        ar[0, :, pl.ds(pl.multiple_of(n * 256, 256), 256)] = code
        return 0

    tr("ig1")
    lax.fori_loop(0, 8, ig_peer, 0)
    ar[0, 6:7, :] = jnp.zeros((1, D), F32)
    for h in range(4):
        ar[0, 6:7, pl.ds(pl.multiple_of(c * HALF + h * DH, DH), DH)] = gain_row[h] + gain_row[4 + h]

    steps = [("c", 0)] + [(a, m) for a in ("x", "y", "z") for m in (0, 1)]

    def small(n):
        axis, m = steps[n]
        i = lax.axis_index(axis)
        partner = 3 - i if m else i + 1 - 2 * lax.rem(i, 2)
        return send(ar.at[n], arr.at[n], arsem.at[0, n], arsem.at[1, n], {axis: partner})

    def small_next(n, cp):
        cp.wait()
        ar[n + 1] = ar[n] + arr[n]
        return small(n + 1) if n + 1 < 7 else None

    small_copy = small(0)
    pl.semaphore_wait(free_sem, 1)
    ig_copy = send(dkv, sqk, igsem.at[0], igsem.at[1], peer)

    def relay(hp):
        axis, d = PLAN[hp]
        mid = product(hp, ring(axis, 1 if d == 1 else 3))
        sends[hp, 0, 0].wait_recv()
        recv[0][0][hp][...] = recv[0][0][hp][...] + mid
        go(hp, 0, 2, recv[0][0][hp], d)

    tr("relay")
    small_copy = small_next(0, small_copy)
    for hp in (0, 1, 2, 3, 4, 5):
        relay(hp)
    tr("own")
    for hp in range(6):
        sends[hp, 0, 0].wait_send()
    for hp in range(6):
        tx[hp][0] = product(hp, ring(PLAN[hp][0], 0))

    tr("ig2")
    small_copy = small_next(1, small_copy)
    ig_copy.wait()

    def ig_own(n, _):
        total = ig_tile(n, c * T, False)
        total = total + jnp.concatenate([sqk[2 * n], sqk[2 * n + 1]], axis=1)
        xb[0, :, pl.ds(pl.multiple_of(n * 256, 256), 256)] = total.astype(BF16)
        return 0

    lax.fori_loop(0, 8, ig_own, 0)
    rg_copy = pltpu.make_async_copy(xb.at[0], rg_hbm, rgsem)
    rg_copy.start()

    def piece(hp, phase, i):
        axis = PLAN[hp][0]
        if phase == 1:
            return tx[hp].at[0, :, :, i] if axis == "y" else tx[hp].at[0, i]
        return t2[hp].at[:, i] if axis == "z" else t2[hp].at[i]

    def ends(hp, phase):
        sends[hp, phase, 1].wait_recv()
        sends[hp, phase, 2].wait_recv()
        return recv[phase][1][hp][...] + recv[phase][2][hp][...]

    tr("ph1a")
    for hp in range(6):
        axis, d = ORDER[PLAN[hp][0]][1], PLAN[hp][1]
        tx[hp][0] = tx[hp][0] + ends(hp, 0)
        go(hp, 1, 0, piece(hp, 1, ring(axis, 2)), d)
        go(hp, 1, 1, piece(hp, 1, ring(axis, 3 if d == 1 else 1)), -d)
        if hp == 1:
            small_copy = small_next(2, small_copy)
    tr("ph1b")
    for hp in range(6):
        axis, d = ORDER[PLAN[hp][0]][1], PLAN[hp][1]
        sends[hp, 1, 0].wait_recv()
        via = recv[1][0][hp]
        via[...] = via[...] + piece(hp, 1, ring(axis, 1 if d == 1 else 3))[...]
        go(hp, 1, 2, via, d)
        if hp == 1:
            small_copy = small_next(3, small_copy)
    small_copy = small_next(4, small_copy)
    tr("ph2a")
    for hp in range(6):
        before, axis = ORDER[PLAN[hp][0]][1:]
        t2[hp][...] = piece(hp, 1, ring(before, 0))[...] + ends(hp, 1)
        for m in range(3):
            sends[hp, 2, m] = send(piece(hp, 2, ring(axis, m + 1)), recv[2][m][hp], sems.at[0, hp, 2, m],
                                   sems.at[1, hp, 2, m], {axis: ring(axis, m + 1)})
    small_copy = small_next(5, small_copy)

    tr("final")
    for hp in range(6):
        sends[hp, 2, 0].wait_recv()
        last = ORDER[PLAN[hp][0]][2]
        fs[:, :, hp * 256 : hp * 256 + 256] = (
            piece(hp, 2, ring(last, 0))[...] + recv[2][0][hp][...] + ends(hp, 2)
        ) * scale
    f_copy = send(fs.at[1 - c], fr, fsem.at[0], fsem.at[1], peer)
    for t in range(3):
        wout[t, :, pl.ds(own_col, HALF)] = fs[c, :, t * HALF : t * HALF + HALF]
    small_next(6, small_copy)
    code_out[...] = ar[7, 0:6, :] * scale
    gain_out[...] = ar[7, 6:7, 0 : 2 * HALF] * scale
    f_copy.wait()
    for t in range(3):
        wout[t, :, pl.ds(peer_col, HALF)] = fr[:, t * HALF : t * HALF + HALF]
    tr("drain")
    for (hp, phase, m), cp in sends.items():
        if (phase, m) != (0, 0):
            cp.wait_send()
    rg_copy.wait()
    tr()


def hand_over(*refs):
    for n in range(4):
        refs[4 + n][...] = refs[n][...]


def vmem(*shape, dtype=F32):
    return pltpu.VMEM(shape, dtype)


def body(resid, token_ids, code_proj, w_query, w_key, w_value, gain, out_grad):
    dma = pltpu.SemaphoreType.DMA
    any_spec = pl.BlockSpec(memory_space=pl.ANY)
    vm = pl.BlockSpec(memory_space=pltpu.VMEM)
    sds = jax.ShapeDtypeStruct
    scale = 1.0 / math.sqrt(T * lax.axis_size(ALL))
    w_out, resid_grad, gain_out, code_out = pl.pallas_call(
        functools.partial(kernel, scale),
        name="layer",
        out_shape=(sds((3, 16, 2 * HALF), F32), sds((T, D), BF16), sds((1, 2 * HALF), F32), sds((6, D), F32)),
        in_specs=[vm] * 3 + [any_spec] * 5,
        out_specs=(vm, any_spec, vm, vm),
        scratch_shapes=[
            vmem(3, D, HALF, dtype=BF16), dma((3,)), vmem(2, T, D, dtype=BF16),
            vmem(8, T, DH, dtype=BF16), vmem(8, T, DH, dtype=BF16), vmem(8, T, DH, dtype=BF16),
            vmem(16, T, DH), vmem(16, T, DH), vmem(8, T, DH, dtype=BF16), dma((9,)),
            vmem(8, T, T, dtype=BF16), vmem(8, T, DH, dtype=BF16),
            vmem(16, T), vmem(16, T), vmem(2, 16, T, dtype=BF16), vmem(3, 16, D, dtype=BF16), vmem(8, 1, DH),
            dma((8,)), dma((8,)), dma((2,)), dma((2,)), pltpu.SemaphoreType.REGULAR,
            vmem(2, 2, 4, DH, DH), vmem(2, 16, 32, DH), vmem(2, 16, 32, DH), vmem(2, 16, 32, DH), vmem(2, 16, 32, DH),
            dma((4, 15)), dma((4, 15)),
            vmem(4, 4, 2, 4, 16, 2 * T, dtype=BF16), vmem(6, 2 * T, 256, dtype=BF16), dma((2,)),
            vmem(8, 8, D), vmem(7, 8, D), dma((2, 7)),
            vmem(2, 16, 3 * HALF), vmem(16, 3 * HALF), dma((2,)), dma,
            dma((2, 6, 3, 3)),
            *[vmem(2, *DIMS[a], 16, 256) for a, _ in PLAN],
            *[vmem(*DIMS2[a], 16, 256) for a, _ in PLAN],
            *[vmem(*DIMS[a], 16, 256) for _ in range(3) for a, _ in PLAN],
            *[vmem(*DIMS2[a], 16, 256) for _ in range(3) for a, _ in PLAN],
            *[vmem(2, 16, 256) for _ in range(3) for a, _ in PLAN],
        ],
        compiler_params=pltpu.CompilerParams(collective_id=0, has_side_effects=True, vmem_limit_bytes=67_043_328),
    )(token_ids, code_proj, gain[None], resid[0], out_grad[0], w_query, w_key, w_value)
    rows = T // 4
    block = pl.BlockSpec((rows, D), lambda i: (i, 0))
    whole = [pl.BlockSpec(shape, lambda i, n=len(shape): (0,) * n) for shape in ((3, 16, 2 * HALF), (1, 2 * HALF), (6, D))]
    resid_grad, w_out, gain_out, code_out = pl.pallas_call(
        hand_over,
        name="hand_over",
        grid=(4,),
        out_shape=(sds((T, D), BF16), sds((3, 16, 2 * HALF), F32), sds((1, 2 * HALF), F32), sds((6, D), F32)),
        in_specs=[block] + whole,
        out_specs=(block, *whole),
    )(resid_grad, w_out, gain_out, code_out)
    return resid_grad[None], w_out.transpose(1, 0, 2), gain_out[0], code_out


def solution(mesh):
    finer = Mesh(mesh.devices.reshape(4, 4, 2, 4), ALL)
    seq = ("z", "y", "c")
    return jax.shard_map(
        body,
        mesh=finer,
        in_specs=(P("x", seq, None), P("x", seq), P(), P(), P(), P(), P(), P("x", seq, None)),
        out_specs=(P("x", seq, None), P(ALL, None, None), P(), P()),
        check_vma=False,
    )
```

```python
import functools
import math

import jax
import jax.numpy as jnp
from jax import lax
from jax.experimental import pallas as pl
from jax.experimental.pallas import tpu as pltpu
from jax.sharding import Mesh
from jax.sharding import PartitionSpec as P

HEADS = 8
DH = 128
T = 512
D = 2048
HALF = 512
ALL = ("z", "y", "c", "x")
MESH = pl.DeviceIdType.MESH
F32 = jnp.float32
BF16 = jnp.bfloat16

fsq_levels = (8, 8, 8, 5, 5, 5)
fsq_bases = (1, 8, 64, 512, 2560, 12800)

NT = (((1,), (1,)), ((), ()))
TN = (((0,), (0,)), ((), ()))


def dot(a, b, dims=None):
    if dims is None:
        return jnp.dot(a, b, preferred_element_type=F32)
    return lax.dot_general(a, b, dims, preferred_element_type=F32)


def entry_signal(devices):
    barrier = pltpu.get_barrier_semaphore()
    for device in devices:
        pl.semaphore_signal(barrier, inc=1, device_id=device, device_id_type=MESH)
    return lambda: pl.semaphore_wait(barrier, len(devices))


def send(src, dst, ssem, rsem, device):
    copy = pltpu.make_async_remote_copy(
        src_ref=src, dst_ref=dst, send_sem=ssem, recv_sem=rsem, device_id=device, device_id_type=MESH
    )
    copy.start()
    return copy


def ring(axis, step):
    return lax.rem(lax.axis_index(axis) + step, 4)


PLAN = (("x", 1), ("x", -1), ("y", 1), ("z", 1), ("y", -1), ("z", -1))
ORDER = {"x": ("x", "z", "y"), "y": ("y", "x", "z"), "z": ("z", "y", "x")}
DIMS = {"x": (4, 4, 2), "y": (4, 2, 4), "z": (4, 2, 4)}
DIMS2 = {"x": (4, 2), "y": (4, 2), "z": (2, 4)}


class Trace:
    on = False
    scope = None

    def __call__(self, name=None):
        if not self.on:
            return
        if self.scope is not None:
            self.scope.__exit__(None, None, None)
        self.scope = jax.named_scope(name) if name else None
        if name:
            self.scope.__enter__()


def kernel(
    scale, ids_ref, proj_ref, gain_ref, resid_hbm, og_hbm, wq_hbm, wk_hbm, wv_hbm,
    wout, rg_hbm, gain_out, code_out,
    wbuf, wsem, xb, q, k, v, sqk, dkv, og, ogsem, sc, datt, nf, ns, nall, proj3, gain_row,
    xssem, xrsem, gsem, nsem, free_sem,
    blk, pre, sbuf, rbuf, obuf, sssem, srsem,
    xt_ref, g_ref, igsem, ar, arr, arsem, asend, agot, asum, aall, got, gotsem, rgsem, sems, *scr,
):
    tr = Trace()

    def pairs(first, last, step):
        def two(i, _):
            step(2 * i)
            step(2 * i + 1)
            return 0

        lax.fori_loop(first // 2, last // 2, two, 0)

    tx, t2 = scr[0:6], scr[6:12]
    recv = [[scr[12 + 18 * phase + 6 * m : 18 + 18 * phase + 6 * m] for m in range(3)] for phase in range(2)]
    c = lax.axis_index("c")
    peer = {"c": 1 - c}
    y = lax.axis_index("y")
    z = lax.axis_index("z")
    own_col = pl.multiple_of(c * HALF, HALF)
    peer_col = pl.multiple_of((1 - c) * HALF, HALF)
    mine = c * 4
    other = (1 - c) * 4

    tr("enter")
    xload = pltpu.make_async_copy(resid_hbm, xb.at[0], ogsem.at[8])
    xload.start()
    loads = []
    for n, w in enumerate((wk_hbm, wv_hbm, wq_hbm)):
        cp = pltpu.make_async_copy(w.at[:, pl.ds(own_col, HALF)], wbuf.at[n], wsem.at[n])
        cp.start()
        loads.append(cp)
    ogloads = []
    for h in range(4):
        for m, (first, col) in enumerate(((other, peer_col), (mine, own_col))):
            cp = pltpu.make_async_copy(
                og_hbm.at[:, pl.ds(pl.multiple_of(col + h * DH, DH), DH)], og.at[first + h], ogsem.at[m * 4 + h])
            cp.start()
            ogloads.append(cp)

    plane = [{"z": ring("z", dz), "y": ring("y", dy)} for dz in range(4) for dy in range(4) if dz or dy]
    plane += [{"x": ring("x", n)} for n in (1, 2, 3)] + [peer]
    plane += [{a: ring(a, n), "c": 1 - c} for a in ("x", "y", "z") for n in (1, 2, 3)]
    all_entered = entry_signal(plane)

    ids = ids_ref[...].astype(F32)
    nf[...] = jnp.zeros_like(nf)
    rest = jnp.zeros((8, D), F32)
    row = lax.broadcasted_iota(jnp.int32, (8, 1), 0)
    inv_level = jnp.zeros((8, 1), F32)
    for j, (level, base) in enumerate(zip(fsq_levels, fsq_bases)):
        quot = jnp.floor((ids + 0.5) * (1.0 / base)) if base > 1 else ids
        digit = quot - level * jnp.floor((quot + 0.5) * (1.0 / level))
        nf[j : j + 1, :] = 2.0 * digit - (level - 1.0)
        inv_level = jnp.where(row == j, 1.0 / (level - 1.0), inv_level)
    proj3[...] = jnp.zeros_like(proj3)
    rest = proj_ref[...] * inv_level[0:6]
    for t in range(3):
        term = rest.astype(BF16)
        proj3[t, 0:6, :] = term
        rest = rest - term.astype(F32)
    nums = nf[...].astype(BF16)
    numt = jnp.concatenate([nums, nums, nums], axis=0)

    tr("inputs")
    xload.wait()
    xcopies = []
    for j in range(8):
        cols = slice(j * 256, j * 256 + 256)
        add = dot(numt, proj3[:, :, cols].reshape(48, 256), TN)
        x = (xb[0, :, cols].astype(F32) + add).astype(BF16)
        xb[0, :, cols] = x
        src, dst = tx[2 + j % 4].at[j // 4], recv[0][1 + j // 4][2 + j % 4]
        src[...] = x.astype(F32).reshape(4, 2, 4, 16, 256)
        if j == 0:
            all_entered()
        xcopies.append(send(src, dst, xssem.at[j], xrsem.at[j], peer))
    for h in range(4):
        ogloads[2 * h].wait()
        dkv[h] = og[other + h].astype(F32)
    g_copy = send(dkv.at[0:4], dkv.at[4:8], gsem.at[0], gsem.at[1], peer)
    n_copy = send(nf, ns, nsem.at[0], nsem.at[1], peer)

    def place(n, at, a):
        if n == 1:
            v[at] = a.astype(BF16)
        else:
            s = 1.0 / (1.0 + jnp.exp(-a))
            slope = s * (1.0 + a * (1.0 - s))
            if n == 0:
                k[at] = (a * s).astype(BF16)
                sqk[8 + at] = slope
            else:
                q[at] = (a * s).astype(BF16)
                sqk[at] = slope

    def project(slot, n, base):
        for half in range(2):
            p = dot(xb[slot], wbuf[n, :, half * 256 : half * 256 + 256])
            for hh in range(2):
                place(n, base + half * 2 + hh, p[:, hh * DH : hh * DH + DH])

    def kv_step(n):
        blk[0, n // 4, lax.rem(n, 4)] = dot(k[n], v[n], TN)

    def kv_steps(base):
        for h in range(4):
            kv_step(base + h)

    tr("own_proj")
    for n in range(2):
        loads[n].wait()
        project(0, n, mine)
    kv_steps(mine)
    for h in range(4):
        ogloads[2 * h + 1].wait()
    tr("peer_kv")
    for part in range(2):
        for j in range(4 * part, 4 * part + 4):
            xcopies[j].wait()
            xb[1, :, j * 256 : j * 256 + 256] = recv[0][1 + j // 4][2 + j % 4][...].reshape(512, 256).astype(BF16)
        ks = slice(part * 1024, part * 1024 + 1024)
        for n in range(2):
            for half in range(2):
                p = dot(xb[1, :, ks], wbuf[n, ks, half * 256 : half * 256 + 256])
                for hh in range(2):
                    a = p[:, hh * DH : hh * DH + DH]
                    h = half * 2 + hh
                    if part == 0:
                        dkv[8 + 4 * n + h] = a
                    else:
                        place(n, other + h, a + dkv[8 + 4 * n + h])

    me = z * 4 + y
    spots = sorted(((dz, dy) for dz in range(4) for dy in range(4) if dz or dy),
                   key=lambda o: -(min(o[0], 4 - o[0]) + min(o[1], 4 - o[1])))

    def to_all(src, dst, n):
        out = []
        for o, (dz, dy) in enumerate(spots):
            zt, yt = ring("z", dz), ring("y", dy)
            out.append(send(src.at[zt * 4 + yt], dst.at[me], sssem.at[n, o], srsem.at[n, o], {"z": zt, "y": yt}))
        return out

    def scan_start(s):
        sbuf[s] = (blk[s, 0] + blk[s, 1]).reshape(16, 32, DH)
        out = to_all(sbuf.at[s], rbuf.at[s], 2 * s)
        rbuf[s, me] = sbuf[s, me]
        return out

    def scan_middle(s, sent):
        for cp in sent:
            cp.wait()
        total = jnp.zeros((32, DH), F32)
        for i in range(16) if s == 0 else reversed(range(16)):
            obuf[s, i] = total
            total = total + rbuf[s, i]
        out = to_all(obuf.at[s], pre.at[s], 2 * s + 1)
        pre[s, me] = obuf[s, me]
        return out

    def scan_end(s, sent):
        for cp in sent:
            cp.wait()

    def state(s, b, h):
        base = pre[s, pl.ds(4 * h, 4)].reshape(DH, DH)
        if s == 0:
            return (base + jnp.where(b == 1, blk[0, 0, h], 0.0)).astype(BF16)
        return (base + jnp.where(b == 0, blk[1, 1, h], 0.0)).astype(BF16)

    tr("kv")
    kv_steps(other)
    sent = scan_start(0)
    tr("qproj")
    loads[2].wait()
    project(0, 2, mine)
    project(1, 2, other)
    g_copy.wait()
    for h in range(4):
        og[other + h] = dkv[4 + h].astype(BF16)
    n_copy.wait()
    nall[c] = nums
    nall[1 - c] = ns[...].astype(BF16)

    row_ids = lax.broadcasted_iota(jnp.int32, (T, T), 0)
    col_ids = lax.broadcasted_iota(jnp.int32, (T, T), 1)

    def score_step(n):
        s = jnp.where(col_ids <= row_ids, dot(q[n], k[n], NT), 0.0).astype(BF16)
        sc[n] = s
        dkv[8 + n] = dot(s, v[n])

    tr("scores1")
    pairs(0, 4, score_step)
    tr("scanmid0")
    sent = scan_middle(0, sent)
    tr("scores2")
    pairs(4, 8, score_step)

    def turn_step(n):
        cols = pl.ds(pl.multiple_of(n * 128, 128), 128)
        for slot in range(2):
            place = c if slot == 0 else 1 - c
            t = xb[slot, :, cols].T
            xt_ref[n // 4, lax.rem(n, 4), :, :, :, pl.ds(pl.multiple_of(place * T, T), T)] = t.reshape(2, 4, 16, T)

    tr("turn")
    pairs(0, 16, turn_step)
    tr("scanend0")
    scan_end(0, sent)

    def forward_step(n):
        b = n // 4
        h = lax.rem(n, 4)
        a = dkv[8 + n] + dot(q[n], state(0, b, h))
        inv = lax.rsqrt(jnp.mean(a * a, axis=-1, keepdims=True) + 1e-06)
        normed = a * inv
        g = og[n].astype(F32)
        dn = g * gain_ref[:, pl.ds(pl.multiple_of(c * HALF + h * DH, DH), DH)]
        da = ((dn - normed * jnp.mean(dn * normed, axis=-1, keepdims=True)) * inv).astype(BF16)
        datt[n] = da
        gain_row[n] = jnp.sum(g * normed, axis=0, keepdims=True)
        blk[1, b, h] = dot(q[n], da, TN)

    tr("fwd")
    pairs(0, 8, forward_step)
    sent = scan_start(1)

    def put(kind, n, value):
        b = n // 4
        h = lax.rem(n, 4)
        g_ref[kind * 2 + h // 2, pl.ds(pl.multiple_of(b * T, T), T),
              pl.ds(pl.multiple_of(lax.rem(h, 2) * DH, DH), DH)] = value.astype(BF16)

    def back_step(n):
        b = n // 4
        h = lax.rem(n, 4)
        da = datt[n]
        bs = jnp.where(col_ids <= row_ids, dot(da, v[n], NT), 0.0).astype(BF16)
        dq = dot(bs, k[n]) + dot(da, state(0, b, h), NT)
        put(0, n, dq * sqk[n])
        dkv[n] = dot(bs, q[n], TN)
        dkv[8 + n] = dot(sc[n], da, TN)

    def lhs(axis, i):
        if axis == "x":
            rows = xt_ref[:, :, :, i]
        elif axis == "y":
            rows = xt_ref[:, i]
        else:
            rows = xt_ref[i]
        return rows.reshape(512, 1024)

    def product(hp, i):
        axis = PLAN[hp][0]
        return dot(lhs(axis, i), g_ref[hp]).reshape(*DIMS[axis], 16, 256)

    sends = {}

    def go(hp, phase, m, src, dirn):
        axis = ORDER[PLAN[hp][0]][phase]
        sends[hp, phase, m] = send(src, recv[phase][m][hp], sems.at[0, hp, phase, m], sems.at[1, hp, phase, m],
                                   {axis: ring(axis, 1 if dirn == 1 else 3)})

    def far(hps):
        for hp in hps:
            tx[hp][0] = product(hp, ring(PLAN[hp][0], 2))
        for hp in hps:
            go(hp, 0, 0, tx[hp].at[0], PLAN[hp][1])

    def straight(hps):
        for hp in hps:
            axis, d = PLAN[hp]
            tx[hp][1] = product(hp, ring(axis, 3 if d == 1 else 1))
        for hp in hps:
            go(hp, 0, 1, tx[hp].at[1], -PLAN[hp][1])

    tr("back1")
    pairs(0, 4, back_step)
    tr("scanmid1")
    sent = scan_middle(1, sent)
    tr("back2")
    pairs(4, 8, back_step)
    tr("xfirst")
    far((0, 1))
    straight((0, 1))
    tr("scanend1")
    scan_end(1, sent)

    def last_step(n):
        st = state(1, n // 4, lax.rem(n, 4))
        put(1, n, (dkv[n] + dot(v[n], st, NT)) * sqk[8 + n])
        put(2, n, dkv[8 + n] + dot(k[n], st))

    tr("last")
    pairs(0, 8, last_step)
    pl.semaphore_signal(free_sem, inc=1, device_id=peer, device_id_type=MESH)
    tr("yzfirst")
    far((2, 3))
    far((4, 5))
    straight((2, 3, 4, 5))

    tr("small")
    smalls = []
    for t in range(3):
        parts = []
        for hp in (2 * t, 2 * t + 1):
            s = dot(nall[0], g_ref[hp, 0:T, :]) + dot(nall[1], g_ref[hp, T : 2 * T, :])
            s = s[0:8] * inv_level
            terms = []
            for _ in range(3):
                term = s.astype(BF16).astype(F32)
                s = s - term
                terms.append(term)
            terms.append(jnp.zeros_like(s))
            parts.append(jnp.concatenate(terms, axis=0))
        smalls.append(jnp.concatenate(parts, axis=1).astype(BF16))

    order_w = (2, 0, 1)

    def ig_tile(n, base, extra):
        total = None
        rows = pl.ds(pl.multiple_of(base, T), T)
        for t in range(3):
            left = jnp.concatenate([g_ref[2 * t, rows, :], g_ref[2 * t + 1, rows, :]], axis=1)
            if extra:
                left = jnp.concatenate([left, smalls[t]], axis=0)
            part = dot(left, wbuf[order_w[t], pl.ds(pl.multiple_of(n * 256, 256), 256), :], NT)
            total = part if total is None else total + part
        return total

    def ig_peer(n, _):
        total = ig_tile(n, (1 - c) * T, True)
        dkv[2 * n] = total[0:T, 0:DH]
        dkv[2 * n + 1] = total[0:T, DH : 2 * DH]
        code = total[T : T + 8] + total[T + 8 : T + 16] + total[T + 16 : T + 24]
        ar[0, :, pl.ds(pl.multiple_of(n * 256, 256), 256)] = code
        return 0

    tr("ig1")
    lax.fori_loop(0, 8, ig_peer, 0)
    ar[0, 6:7, :] = jnp.zeros((1, D), F32)
    for h in range(4):
        ar[0, 6:7, pl.ds(pl.multiple_of(c * HALF + h * DH, DH), DH)] = gain_row[h] + gain_row[4 + h]

    steps = (("c", 0), ("x", 0), ("x", 1))

    def small(n):
        axis, m = steps[n]
        i = lax.axis_index(axis)
        partner = 3 - i if m else i + 1 - 2 * lax.rem(i, 2)
        return send(ar.at[n], arr.at[n], arsem.at[0, n], arsem.at[1, n], {axis: partner})

    def small_next(n, cp):
        cp.wait()
        ar[n + 1] = ar[n] + arr[n]
        return small(n + 1) if n + 1 < 3 else None

    def plane_gather():
        for i in range(16):
            asend[i] = ar[3, :, i * 128 : i * 128 + 128]
        agot[me] = asend[me]
        return to_all(asend, agot, 4)

    def plane_return(sent):
        for cp in sent:
            cp.wait()
        total = agot[0]
        for i in range(1, 16):
            total = total + agot[i]
        asum[...] = total
        aall[me] = total
        out = []
        for o, (dz, dy) in enumerate(spots):
            out.append(send(asum, aall.at[me], sssem.at[5, o], srsem.at[5, o], {"z": ring("z", dz), "y": ring("y", dy)}))
        return out

    small_copy = small(0)
    pl.semaphore_wait(free_sem, 1)
    ig_copy = send(dkv, sqk, igsem.at[0], igsem.at[1], peer)

    def relay(hp):
        axis, d = PLAN[hp]
        mid = product(hp, ring(axis, 1 if d == 1 else 3))
        sends[hp, 0, 0].wait_recv()
        recv[0][0][hp][...] = recv[0][0][hp][...] + mid
        go(hp, 0, 2, recv[0][0][hp], d)

    tr("relay")
    small_copy = small_next(0, small_copy)
    for hp in (0, 1, 2, 3, 4, 5):
        relay(hp)
    tr("own")
    for hp in range(6):
        sends[hp, 0, 0].wait_send()
    for hp in range(6):
        tx[hp][0] = product(hp, ring(PLAN[hp][0], 0))

    tr("ig2")
    small_copy = small_next(1, small_copy)
    ig_copy.wait()

    def ig_own(n, _):
        total = ig_tile(n, c * T, False)
        total = total + jnp.concatenate([sqk[2 * n], sqk[2 * n + 1]], axis=1)
        xb[0, :, pl.ds(pl.multiple_of(n * 256, 256), 256)] = total.astype(BF16)
        return 0

    lax.fori_loop(0, 8, ig_own, 0)
    rg_copy = pltpu.make_async_copy(xb.at[0], rg_hbm, rgsem)
    rg_copy.start()

    def piece(hp, phase, i):
        axis = PLAN[hp][0]
        if phase == 1:
            return tx[hp].at[0, :, :, i] if axis == "y" else tx[hp].at[0, i]
        return t2[hp].at[:, i] if axis == "z" else t2[hp].at[i]

    def ends(hp, phase):
        sends[hp, phase, 1].wait_recv()
        sends[hp, phase, 2].wait_recv()
        return recv[phase][1][hp][...] + recv[phase][2][hp][...]

    def first(hp):
        go(hp, 1, 0, piece(hp, 1, ring(ORDER[PLAN[hp][0]][1], 2)), PLAN[hp][1])

    def second(hp):
        d = PLAN[hp][1]
        go(hp, 1, 1, piece(hp, 1, ring(ORDER[PLAN[hp][0]][1], 3 if d == 1 else 1)), -d)

    tr("ph1a")
    for hp in range(6):
        tx[hp][0] = tx[hp][0] + ends(hp, 0)
        first(hp)
        if hp == 1:
            second(0)
            second(1)
            small_next(2, small_copy)
            small_sent = plane_gather()
    for hp in range(2, 6):
        second(hp)
    tr("ph1b")
    for hp in range(6):
        axis, d = ORDER[PLAN[hp][0]][1], PLAN[hp][1]
        sends[hp, 1, 0].wait_recv()
        via = recv[1][0][hp]
        via[...] = via[...] + piece(hp, 1, ring(axis, 1 if d == 1 else 3))[...]
        go(hp, 1, 2, via, d)
    small_sent = plane_return(small_sent)
    tr("ph2a")
    for hp in range(6):
        prior, axis = ORDER[PLAN[hp][0]][1:]
        t2[hp][...] = piece(hp, 1, ring(prior, 0))[...] + ends(hp, 1)
        for m in (2, 1, 3, 0):
            for rel in (0, 1) if m else (1,):
                device = {axis: ring(axis, m), "c": c if rel == 0 else 1 - c} if m else peer
                if m and rel == 0:
                    device = {axis: ring(axis, m)}
                sends[hp, 2, (m, rel)] = send(
                    piece(hp, 2, ring(axis, m)).at[c if rel == 0 else 1 - c], got.at[hp, rel, m],
                    gotsem.at[0, hp, rel, m], gotsem.at[1, hp, rel, m], device)

    tr("final")
    for hp in range(6):
        for m in range(4):
            for rel in (0, 1) if m else (1,):
                sends[hp, 2, (m, rel)].wait_recv()
        last = ORDER[PLAN[hp][0]][2]
        own_sum = piece(hp, 2, ring(last, 0)).at[c][...] + got[hp, 0, 1] + got[hp, 0, 2] + got[hp, 0, 3]
        peer_sum = got[hp, 1, 0] + got[hp, 1, 1] + got[hp, 1, 2] + got[hp, 1, 3]
        shift = (hp % 2) * 256
        wout[hp // 2, :, pl.ds(pl.multiple_of(c * HALF + shift, 256), 256)] = own_sum * scale
        wout[hp // 2, :, pl.ds(pl.multiple_of((1 - c) * HALF + shift, 256), 256)] = peer_sum * scale
    for cp in small_sent:
        cp.wait()
    for i in range(16):
        code_out[:, i * 128 : i * 128 + 128] = aall[i, 0:6] * scale
        if i < 8:
            gain_out[:, i * 128 : i * 128 + 128] = aall[i, 6:7] * scale
    tr("drain")
    for (hp, phase, m), cp in sends.items():
        if (phase, m) != (0, 0):
            cp.wait_send()
    rg_copy.wait()
    tr()


def hand_over(*refs):
    ins, outs, bufs, sem = refs[:4], refs[4:8], refs[8:12], refs[12]
    parts = [(0, pl.ds(r * 128, 128)) for r in range(4)] + [(n, slice(None)) for n in (1, 2, 3)]
    loads = []
    for i, (n, rows) in enumerate(parts):
        loads.append(pltpu.make_async_copy(ins[n].at[rows], bufs[n].at[rows], sem.at[0, i]))
        loads[-1].start()
    stores = []
    for i, (n, rows) in enumerate(parts):
        loads[i].wait()
        stores.append(pltpu.make_async_copy(bufs[n].at[rows], outs[n].at[rows], sem.at[1, i]))
        stores[-1].start()
    for cp in stores:
        cp.wait()


def vmem(*shape, dtype=F32):
    return pltpu.VMEM(shape, dtype)


def body(resid, token_ids, code_proj, w_query, w_key, w_value, gain, out_grad):
    dma = pltpu.SemaphoreType.DMA
    any_spec = pl.BlockSpec(memory_space=pl.ANY)
    vm = pl.BlockSpec(memory_space=pltpu.VMEM)
    sds = jax.ShapeDtypeStruct
    scale = 1.0 / math.sqrt(T * lax.axis_size(ALL))
    w_out, resid_grad, gain_out, code_out = pl.pallas_call(
        functools.partial(kernel, scale),
        name="layer",
        out_shape=(sds((3, 16, 2 * HALF), F32), sds((T, D), BF16), sds((1, 2 * HALF), F32), sds((6, D), F32)),
        in_specs=[vm] * 3 + [any_spec] * 5,
        out_specs=(vm, any_spec, vm, vm),
        scratch_shapes=[
            vmem(3, D, HALF, dtype=BF16), dma((3,)), vmem(2, T, D, dtype=BF16),
            vmem(8, T, DH, dtype=BF16), vmem(8, T, DH, dtype=BF16), vmem(8, T, DH, dtype=BF16),
            vmem(16, T, DH), vmem(16, T, DH), vmem(8, T, DH, dtype=BF16), dma((9,)),
            vmem(8, T, T, dtype=BF16), vmem(8, T, DH, dtype=BF16),
            vmem(16, T), vmem(16, T), vmem(2, 16, T, dtype=BF16), vmem(3, 16, D, dtype=BF16), vmem(8, 1, DH),
            dma((8,)), dma((8,)), dma((2,)), dma((2,)), pltpu.SemaphoreType.REGULAR,
            vmem(2, 2, 4, DH, DH), vmem(2, 16, 32, DH), vmem(2, 16, 32, DH), vmem(2, 16, 32, DH), vmem(2, 16, 32, DH),
            dma((6, 15)), dma((6, 15)),
            vmem(4, 4, 2, 4, 16, 2 * T, dtype=BF16), vmem(6, 2 * T, 256, dtype=BF16), dma((2,)),
            vmem(4, 8, D), vmem(3, 8, D), dma((2, 3)),
            vmem(16, 8, DH), vmem(16, 8, DH), vmem(8, DH), vmem(16, 8, DH),
            vmem(6, 2, 4, 16, 256), dma((2, 6, 2, 4)), dma,
            dma((2, 6, 2, 3)),
            *[vmem(2, *DIMS[a], 16, 256) for a, _ in PLAN],
            *[vmem(*DIMS2[a], 16, 256) for a, _ in PLAN],
            *[vmem(*DIMS[a], 16, 256) for _ in range(3) for a, _ in PLAN],
            *[vmem(*DIMS2[a], 16, 256) for _ in range(3) for a, _ in PLAN],
        ],
        compiler_params=pltpu.CompilerParams(collective_id=0, has_side_effects=True, vmem_limit_bytes=67_043_328),
    )(token_ids, code_proj, gain[None], resid[0], out_grad[0], w_query, w_key, w_value)
    shapes = (sds((T, D), BF16), sds((3, 16, 2 * HALF), F32), sds((1, 2 * HALF), F32), sds((6, D), F32))
    resid_grad, w_out, gain_out, code_out = pl.pallas_call(
        hand_over,
        name="hand_over",
        out_shape=shapes,
        in_specs=[any_spec] * 4,
        out_specs=[any_spec] * 4,
        scratch_shapes=[*[vmem(*n.shape, dtype=n.dtype) for n in shapes], dma((2, 7))],
    )(resid_grad, w_out, gain_out, code_out)
    return resid_grad[None], w_out.transpose(1, 0, 2), gain_out[0], code_out


def solution(mesh):
    finer = Mesh(mesh.devices.reshape(4, 4, 2, 4), ALL)
    seq = ("z", "y", "c")
    return jax.shard_map(
        body,
        mesh=finer,
        in_specs=(P("x", seq, None), P("x", seq), P(), P(), P(), P(), P(), P("x", seq, None)),
        out_specs=(P("x", seq, None), P(ALL, None, None), P(), P()),
        check_vma=False,
    )
```

```python
import functools
import math

import jax
import jax.numpy as jnp
from jax import lax
from jax.experimental import pallas as pl
from jax.experimental.pallas import tpu as pltpu
from jax.sharding import Mesh
from jax.sharding import PartitionSpec as P

HEADS = 8
DH = 128
T = 512
D = 2048
HALF = 512
ALL = ("z", "y", "c", "x")
MESH = pl.DeviceIdType.MESH
F32 = jnp.float32
BF16 = jnp.bfloat16

fsq_levels = (8, 8, 8, 5, 5, 5)
fsq_bases = (1, 8, 64, 512, 2560, 12800)

NT = (((1,), (1,)), ((), ()))
TN = (((0,), (0,)), ((), ()))


def dot(a, b, dims=None):
    if dims is None:
        return jnp.dot(a, b, preferred_element_type=F32)
    return lax.dot_general(a, b, dims, preferred_element_type=F32)


def entry_signal(devices):
    barrier = pltpu.get_barrier_semaphore()
    for device in devices:
        pl.semaphore_signal(barrier, inc=1, device_id=device, device_id_type=MESH)
    return lambda: pl.semaphore_wait(barrier, len(devices))


def send(src, dst, ssem, rsem, device):
    copy = pltpu.make_async_remote_copy(
        src_ref=src, dst_ref=dst, send_sem=ssem, recv_sem=rsem, device_id=device, device_id_type=MESH
    )
    copy.start()
    return copy


def ring(axis, step):
    return lax.rem(lax.axis_index(axis) + step, 4)


PLAN = (("x", 1), ("x", -1), ("y", 1), ("z", 1), ("y", -1), ("z", -1))
ORDER = {"x": ("x", "z", "y"), "y": ("y", "x", "z"), "z": ("z", "y", "x")}
DIMS = {"x": (4, 4, 2), "y": (4, 2, 4), "z": (4, 2, 4)}
DIMS2 = {"x": (4, 2), "y": (4, 2), "z": (2, 4)}


class Trace:
    on = False
    scope = None

    def __call__(self, name=None):
        if not self.on:
            return
        if self.scope is not None:
            self.scope.__exit__(None, None, None)
        self.scope = jax.named_scope(name) if name else None
        if name:
            self.scope.__enter__()


def kernel(
    scale, ids_hbm, proj_hbm, gain_hbm, resid_hbm, og_hbm, wq_hbm, wk_hbm, wv_hbm,
    wout, rg_hbm, gain_out, code_out,
    ids_ref, proj_ref, gain_ref, opsem, wbuf, wsem, xb, q, k, v, sqk, dkv, og, ogsem, sc, datt, nf, ns, nall, proj3, gain_row,
    xssem, xrsem, gsem, nsem, free_sem,
    blk, pre, sbuf, rbuf, obuf, sssem, srsem,
    xt_ref, g_ref, igsem, ar, arr, arsem, asend, agot, asum, aall, got, gotsem, rgsem, sems, *scr,
):
    tr = Trace()

    def pairs(first, last, step):
        def two(i, _):
            step(2 * i)
            step(2 * i + 1)
            return 0

        lax.fori_loop(first // 2, last // 2, two, 0)

    tx, t2 = scr[0:6], scr[6:12]
    recv = [[scr[12 + 18 * phase + 6 * m : 18 + 18 * phase + 6 * m] for m in range(3)] for phase in range(2)]
    c = lax.axis_index("c")
    peer = {"c": 1 - c}
    y = lax.axis_index("y")
    z = lax.axis_index("z")
    own_col = pl.multiple_of(c * HALF, HALF)
    peer_col = pl.multiple_of((1 - c) * HALF, HALF)
    mine = c * 4
    other = (1 - c) * 4

    tr("enter")
    small_loads = []
    for n, (src, dst) in enumerate(((ids_hbm, ids_ref), (proj_hbm, proj_ref), (gain_hbm, gain_ref))):
        small_loads.append(pltpu.make_async_copy(src, dst, opsem.at[n]))
        small_loads[-1].start()
    xloads = []
    for n in range(4):
        cols = pl.ds(n * 512, 512)
        xloads.append(pltpu.make_async_copy(resid_hbm.at[:, cols], xb.at[0, :, cols], opsem.at[3 + n]))
        xloads[-1].start()
    loads = [
        pltpu.make_async_copy(w.at[:, pl.ds(own_col, HALF)], wbuf.at[n], wsem.at[n])
        for n, w in enumerate((wk_hbm, wv_hbm, wq_hbm))
    ]
    ogloads = []
    for h in range(4):
        for m, (first, col) in enumerate(((other, peer_col), (mine, own_col))):
            ogloads.append(pltpu.make_async_copy(
                og_hbm.at[:, pl.ds(pl.multiple_of(col + h * DH, DH), DH)], og.at[first + h], ogsem.at[m * 4 + h]))

    plane = [{"z": ring("z", dz), "y": ring("y", dy)} for dz in range(4) for dy in range(4) if dz or dy]
    plane += [{"x": ring("x", n)} for n in (1, 2, 3)] + [peer]
    plane += [{a: ring(a, n), "c": 1 - c} for a in ("x", "y", "z") for n in (1, 2, 3)]
    all_entered = entry_signal(plane)

    for cp in small_loads:
        cp.wait()
    ids = ids_ref[...].astype(F32)
    nf[...] = jnp.zeros_like(nf)
    rest = jnp.zeros((8, D), F32)
    row = lax.broadcasted_iota(jnp.int32, (8, 1), 0)
    inv_level = jnp.zeros((8, 1), F32)
    for j, (level, base) in enumerate(zip(fsq_levels, fsq_bases)):
        quot = jnp.floor((ids + 0.5) * (1.0 / base)) if base > 1 else ids
        digit = quot - level * jnp.floor((quot + 0.5) * (1.0 / level))
        nf[j : j + 1, :] = 2.0 * digit - (level - 1.0)
        inv_level = jnp.where(row == j, 1.0 / (level - 1.0), inv_level)
    proj3[...] = jnp.zeros_like(proj3)
    rest = proj_ref[...] * inv_level[0:6]
    for t in range(3):
        term = rest.astype(BF16)
        proj3[t, 0:6, :] = term
        rest = rest - term.astype(F32)
    nums = nf[...].astype(BF16)
    numt = jnp.concatenate([nums, nums, nums], axis=0)

    tr("inputs")
    xcopies = []
    for j in range(8):
        if j % 2 == 0:
            xloads[j // 2].wait()
        if j == 2:
            for cp in loads + ogloads:
                cp.start()
        cols = slice(j * 256, j * 256 + 256)
        add = dot(numt, proj3[:, :, cols].reshape(48, 256), TN)
        x = (xb[0, :, cols].astype(F32) + add).astype(BF16)
        xb[0, :, cols] = x
        src, dst = tx[2 + j % 4].at[j // 4], recv[0][1 + j // 4][2 + j % 4]
        src[...] = x.astype(F32).reshape(4, 2, 4, 16, 256)
        if j == 0:
            all_entered()
        xcopies.append(send(src, dst, xssem.at[j], xrsem.at[j], peer))
    for h in range(4):
        ogloads[2 * h].wait()
        dkv[h] = og[other + h].astype(F32)
    g_copy = send(dkv.at[0:4], dkv.at[4:8], gsem.at[0], gsem.at[1], peer)
    n_copy = send(nf, ns, nsem.at[0], nsem.at[1], peer)

    def place(n, at, a):
        if n == 1:
            v[at] = a.astype(BF16)
        else:
            s = 1.0 / (1.0 + jnp.exp(-a))
            slope = s * (1.0 + a * (1.0 - s))
            if n == 0:
                k[at] = (a * s).astype(BF16)
                sqk[8 + at] = slope
            else:
                q[at] = (a * s).astype(BF16)
                sqk[at] = slope

    def project(slot, n, base):
        for half in range(2):
            p = dot(xb[slot], wbuf[n, :, half * 256 : half * 256 + 256])
            for hh in range(2):
                place(n, base + half * 2 + hh, p[:, hh * DH : hh * DH + DH])

    def kv_step(n):
        blk[0, n // 4, lax.rem(n, 4)] = dot(k[n], v[n], TN)

    def kv_steps(base):
        for h in range(4):
            kv_step(base + h)

    tr("own_proj")
    for n in range(2):
        loads[n].wait()
        project(0, n, mine)
    kv_steps(mine)
    for h in range(4):
        ogloads[2 * h + 1].wait()
    tr("peer_kv")
    for part in range(2):
        for j in range(4 * part, 4 * part + 4):
            xcopies[j].wait()
            xb[1, :, j * 256 : j * 256 + 256] = recv[0][1 + j // 4][2 + j % 4][...].reshape(512, 256).astype(BF16)
        ks = slice(part * 1024, part * 1024 + 1024)
        for n in range(2):
            for half in range(2):
                p = dot(xb[1, :, ks], wbuf[n, ks, half * 256 : half * 256 + 256])
                for hh in range(2):
                    a = p[:, hh * DH : hh * DH + DH]
                    h = half * 2 + hh
                    if part == 0:
                        dkv[8 + 4 * n + h] = a
                    else:
                        place(n, other + h, a + dkv[8 + 4 * n + h])

    me = z * 4 + y
    spots = sorted(((dz, dy) for dz in range(4) for dy in range(4) if dz or dy),
                   key=lambda o: -(min(o[0], 4 - o[0]) + min(o[1], 4 - o[1])))

    def to_all(src, dst, n):
        out = []
        for o, (dz, dy) in enumerate(spots):
            zt, yt = ring("z", dz), ring("y", dy)
            out.append(send(src.at[zt * 4 + yt], dst.at[me], sssem.at[n, o], srsem.at[n, o], {"z": zt, "y": yt}))
        return out

    def scan_start(s):
        sbuf[s] = (blk[s, 0] + blk[s, 1]).reshape(16, 32, DH)
        out = to_all(sbuf.at[s], rbuf.at[s], 2 * s)
        rbuf[s, me] = sbuf[s, me]
        return out

    def scan_middle(s, sent):
        for cp in sent:
            cp.wait()
        total = jnp.zeros((32, DH), F32)
        for i in range(16) if s == 0 else reversed(range(16)):
            obuf[s, i] = total
            total = total + rbuf[s, i]
        out = to_all(obuf.at[s], pre.at[s], 2 * s + 1)
        pre[s, me] = obuf[s, me]
        return out

    def scan_end(s, sent):
        for cp in sent:
            cp.wait()

    def state(s, b, h):
        base = pre[s, pl.ds(4 * h, 4)].reshape(DH, DH)
        if s == 0:
            return (base + jnp.where(b == 1, blk[0, 0, h], 0.0)).astype(BF16)
        return (base + jnp.where(b == 0, blk[1, 1, h], 0.0)).astype(BF16)

    tr("kv")
    kv_steps(other)
    sent = scan_start(0)
    tr("qproj")
    loads[2].wait()
    project(0, 2, mine)
    project(1, 2, other)
    g_copy.wait()
    for h in range(4):
        og[other + h] = dkv[4 + h].astype(BF16)
    n_copy.wait()
    nall[c] = nums
    nall[1 - c] = ns[...].astype(BF16)

    row_ids = lax.broadcasted_iota(jnp.int32, (T, T), 0)
    col_ids = lax.broadcasted_iota(jnp.int32, (T, T), 1)

    def score_step(n):
        s = jnp.where(col_ids <= row_ids, dot(q[n], k[n], NT), 0.0).astype(BF16)
        sc[n] = s
        dkv[8 + n] = dot(s, v[n])

    tr("scores1")
    pairs(0, 4, score_step)
    tr("scanmid0")
    sent = scan_middle(0, sent)
    tr("scores2")
    pairs(4, 8, score_step)

    def turn_step(n):
        cols = pl.ds(pl.multiple_of(n * 128, 128), 128)
        for slot in range(2):
            place = c if slot == 0 else 1 - c
            t = xb[slot, :, cols].T
            xt_ref[n // 4, lax.rem(n, 4), :, :, :, pl.ds(pl.multiple_of(place * T, T), T)] = t.reshape(2, 4, 16, T)

    tr("turn")
    pairs(0, 16, turn_step)
    tr("scanend0")
    scan_end(0, sent)

    def forward_step(n):
        b = n // 4
        h = lax.rem(n, 4)
        a = dkv[8 + n] + dot(q[n], state(0, b, h))
        g = og[n].astype(F32)
        dn = g * gain_ref[:, pl.ds(pl.multiple_of(c * HALF + h * DH, DH), DH)]
        square = jnp.sum(a * a, axis=-1, keepdims=True)
        cross = jnp.sum(dn * a, axis=-1, keepdims=True)
        inv = lax.rsqrt(square * (1.0 / DH) + 1e-06)
        normed = a * inv
        da = (dn * inv - normed * ((cross * inv) * (inv * (1.0 / DH)))).astype(BF16)
        datt[n] = da
        gain_row[n] = jnp.sum(g * normed, axis=0, keepdims=True)
        blk[1, b, h] = dot(q[n], da, TN)

    tr("fwd")
    pairs(0, 8, forward_step)
    sent = scan_start(1)

    def put(kind, n, value):
        b = n // 4
        h = lax.rem(n, 4)
        g_ref[kind * 2 + h // 2, pl.ds(pl.multiple_of(b * T, T), T),
              pl.ds(pl.multiple_of(lax.rem(h, 2) * DH, DH), DH)] = value.astype(BF16)

    def back_step(n):
        b = n // 4
        h = lax.rem(n, 4)
        da = datt[n]
        bs = jnp.where(col_ids <= row_ids, dot(da, v[n], NT), 0.0).astype(BF16)
        dq = dot(bs, k[n]) + dot(da, state(0, b, h), NT)
        put(0, n, dq * sqk[n])
        dkv[n] = dot(bs, q[n], TN)
        dkv[8 + n] = dot(sc[n], da, TN)

    def lhs(axis, i):
        if axis == "x":
            rows = xt_ref[:, :, :, i]
        elif axis == "y":
            rows = xt_ref[:, i]
        else:
            rows = xt_ref[i]
        return rows.reshape(512, 1024)

    def product(hp, i):
        axis = PLAN[hp][0]
        return dot(lhs(axis, i), g_ref[hp]).reshape(*DIMS[axis], 16, 256)

    sends = {}

    def go(hp, phase, m, src, dirn):
        axis = ORDER[PLAN[hp][0]][phase]
        sends[hp, phase, m] = send(src, recv[phase][m][hp], sems.at[0, hp, phase, m], sems.at[1, hp, phase, m],
                                   {axis: ring(axis, 1 if dirn == 1 else 3)})

    def far(hps):
        for hp in hps:
            tx[hp][0] = product(hp, ring(PLAN[hp][0], 2))
        for hp in hps:
            go(hp, 0, 0, tx[hp].at[0], PLAN[hp][1])

    def straight(hps):
        for hp in hps:
            axis, d = PLAN[hp]
            tx[hp][1] = product(hp, ring(axis, 3 if d == 1 else 1))
        for hp in hps:
            go(hp, 0, 1, tx[hp].at[1], -PLAN[hp][1])

    tr("back1")
    pairs(0, 4, back_step)
    tr("scanmid1")
    sent = scan_middle(1, sent)
    tr("back2")
    pairs(4, 8, back_step)
    tr("xfirst")
    far((0, 1))
    straight((0, 1))
    tr("scanend1")
    scan_end(1, sent)

    def last_step(n):
        st = state(1, n // 4, lax.rem(n, 4))
        put(1, n, (dkv[n] + dot(v[n], st, NT)) * sqk[8 + n])
        put(2, n, dkv[8 + n] + dot(k[n], st))

    tr("last")
    pairs(0, 8, last_step)
    pl.semaphore_signal(free_sem, inc=1, device_id=peer, device_id_type=MESH)
    tr("yzfirst")
    far((2, 3))
    far((4, 5))
    straight((2, 3, 4, 5))

    tr("small")
    smalls = []
    for t in range(3):
        parts = []
        for hp in (2 * t, 2 * t + 1):
            s = dot(nall[0], g_ref[hp, 0:T, :]) + dot(nall[1], g_ref[hp, T : 2 * T, :])
            s = s[0:8] * inv_level
            terms = []
            for _ in range(3):
                term = s.astype(BF16).astype(F32)
                s = s - term
                terms.append(term)
            terms.append(jnp.zeros_like(s))
            parts.append(jnp.concatenate(terms, axis=0))
        smalls.append(jnp.concatenate(parts, axis=1).astype(BF16))

    order_w = (2, 0, 1)

    def ig_tile(n, base, extra):
        total = None
        rows = pl.ds(pl.multiple_of(base, T), T)
        for t in range(3):
            left = jnp.concatenate([g_ref[2 * t, rows, :], g_ref[2 * t + 1, rows, :]], axis=1)
            if extra:
                left = jnp.concatenate([left, smalls[t]], axis=0)
            part = dot(left, wbuf[order_w[t], pl.ds(pl.multiple_of(n * 256, 256), 256), :], NT)
            total = part if total is None else total + part
        return total

    def ig_peer(n, _):
        total = ig_tile(n, (1 - c) * T, True)
        dkv[2 * n] = total[0:T, 0:DH]
        dkv[2 * n + 1] = total[0:T, DH : 2 * DH]
        code = total[T : T + 8] + total[T + 8 : T + 16] + total[T + 16 : T + 24]
        ar[0, :, pl.ds(pl.multiple_of(n * 256, 256), 256)] = code
        return 0

    tr("ig1")
    lax.fori_loop(0, 8, ig_peer, 0)
    ar[0, 6:7, :] = jnp.zeros((1, D), F32)
    for h in range(4):
        ar[0, 6:7, pl.ds(pl.multiple_of(c * HALF + h * DH, DH), DH)] = gain_row[h] + gain_row[4 + h]

    steps = (("c", 0), ("x", 0), ("x", 1))

    def small(n):
        axis, m = steps[n]
        i = lax.axis_index(axis)
        partner = 3 - i if m else i + 1 - 2 * lax.rem(i, 2)
        return send(ar.at[n], arr.at[n], arsem.at[0, n], arsem.at[1, n], {axis: partner})

    def small_next(n, cp):
        cp.wait()
        ar[n + 1] = ar[n] + arr[n]
        return small(n + 1) if n + 1 < 3 else None

    def plane_gather():
        for i in range(16):
            asend[i] = ar[3, :, i * 128 : i * 128 + 128]
        agot[me] = asend[me]
        return to_all(asend, agot, 4)

    def plane_return(sent):
        for cp in sent:
            cp.wait()
        total = agot[0]
        for i in range(1, 16):
            total = total + agot[i]
        asum[...] = total
        aall[me] = total
        out = []
        for o, (dz, dy) in enumerate(spots):
            out.append(send(asum, aall.at[me], sssem.at[5, o], srsem.at[5, o], {"z": ring("z", dz), "y": ring("y", dy)}))
        return out

    small_copy = small(0)
    pl.semaphore_wait(free_sem, 1)
    ig_copy = send(dkv, sqk, igsem.at[0], igsem.at[1], peer)

    def relay(hp):
        axis, d = PLAN[hp]
        mid = product(hp, ring(axis, 1 if d == 1 else 3))
        sends[hp, 0, 0].wait_recv()
        recv[0][0][hp][...] = recv[0][0][hp][...] + mid
        go(hp, 0, 2, recv[0][0][hp], d)

    tr("relay")
    small_copy = small_next(0, small_copy)
    for hp in (0, 1, 2, 3, 4, 5):
        relay(hp)
    tr("own")
    for hp in range(6):
        sends[hp, 0, 0].wait_send()
    for hp in range(6):
        tx[hp][0] = product(hp, ring(PLAN[hp][0], 0))

    tr("ig2")
    small_copy = small_next(1, small_copy)
    ig_copy.wait()

    def ig_own(n, _):
        total = ig_tile(n, c * T, False)
        total = total + jnp.concatenate([sqk[2 * n], sqk[2 * n + 1]], axis=1)
        xb[0, :, pl.ds(pl.multiple_of(n * 256, 256), 256)] = total.astype(BF16)
        return 0

    lax.fori_loop(0, 8, ig_own, 0)
    rg_copy = pltpu.make_async_copy(xb.at[0], rg_hbm, rgsem)
    rg_copy.start()

    def piece(hp, phase, i):
        axis = PLAN[hp][0]
        if phase == 1:
            return tx[hp].at[0, :, :, i] if axis == "y" else tx[hp].at[0, i]
        return t2[hp].at[:, i] if axis == "z" else t2[hp].at[i]

    def ends(hp, phase):
        sends[hp, phase, 1].wait_recv()
        sends[hp, phase, 2].wait_recv()
        return recv[phase][1][hp][...] + recv[phase][2][hp][...]

    def first(hp):
        go(hp, 1, 0, piece(hp, 1, ring(ORDER[PLAN[hp][0]][1], 2)), PLAN[hp][1])

    def second(hp):
        d = PLAN[hp][1]
        go(hp, 1, 1, piece(hp, 1, ring(ORDER[PLAN[hp][0]][1], 3 if d == 1 else 1)), -d)

    tr("ph1a")
    for hp in range(6):
        tx[hp][0] = tx[hp][0] + ends(hp, 0)
        first(hp)
        if hp == 1:
            second(0)
            second(1)
            small_next(2, small_copy)
            small_sent = plane_gather()
    for hp in range(2, 6):
        second(hp)
    tr("ph1b")
    for hp in range(6):
        axis, d = ORDER[PLAN[hp][0]][1], PLAN[hp][1]
        sends[hp, 1, 0].wait_recv()
        via = recv[1][0][hp]
        via[...] = via[...] + piece(hp, 1, ring(axis, 1 if d == 1 else 3))[...]
        go(hp, 1, 2, via, d)
    small_sent = plane_return(small_sent)
    tr("ph2a")
    for hp in range(6):
        prior, axis = ORDER[PLAN[hp][0]][1:]
        t2[hp][...] = piece(hp, 1, ring(prior, 0))[...] + ends(hp, 1)
        for m in (2, 1, 3, 0):
            for rel in (0, 1) if m else (1,):
                device = {axis: ring(axis, m), "c": c if rel == 0 else 1 - c} if m else peer
                if m and rel == 0:
                    device = {axis: ring(axis, m)}
                sends[hp, 2, (m, rel)] = send(
                    piece(hp, 2, ring(axis, m)).at[c if rel == 0 else 1 - c], got.at[hp, rel, m],
                    gotsem.at[0, hp, rel, m], gotsem.at[1, hp, rel, m], device)

    tr("final")
    for hp in range(6):
        for m in range(4):
            for rel in (0, 1) if m else (1,):
                sends[hp, 2, (m, rel)].wait_recv()
        last = ORDER[PLAN[hp][0]][2]
        own_sum = piece(hp, 2, ring(last, 0)).at[c][...] + got[hp, 0, 1] + got[hp, 0, 2] + got[hp, 0, 3]
        peer_sum = got[hp, 1, 0] + got[hp, 1, 1] + got[hp, 1, 2] + got[hp, 1, 3]
        shift = (hp % 2) * 256
        wout[hp // 2, :, pl.ds(pl.multiple_of(c * HALF + shift, 256), 256)] = own_sum * scale
        wout[hp // 2, :, pl.ds(pl.multiple_of((1 - c) * HALF + shift, 256), 256)] = peer_sum * scale
    for cp in small_sent:
        cp.wait()
    for i in range(16):
        code_out[:, i * 128 : i * 128 + 128] = aall[i, 0:6] * scale
        if i < 8:
            gain_out[:, i * 128 : i * 128 + 128] = aall[i, 6:7] * scale
    tr("drain")
    for (hp, phase, m), cp in sends.items():
        if (phase, m) != (0, 0):
            cp.wait_send()
    rg_copy.wait()
    tr()


def hand_over(*refs):
    ins, outs, bufs, sem = refs[:4], refs[4:8], refs[8:12], refs[12]
    parts = [(0, pl.ds(r * 128, 128)) for r in range(4)] + [(n, slice(None)) for n in (1, 2, 3)]
    loads = []
    for i, (n, rows) in enumerate(parts):
        loads.append(pltpu.make_async_copy(ins[n].at[rows], bufs[n].at[rows], sem.at[0, i]))
        loads[-1].start()
    stores = []
    for i, (n, rows) in enumerate(parts):
        loads[i].wait()
        stores.append(pltpu.make_async_copy(bufs[n].at[rows], outs[n].at[rows], sem.at[1, i]))
        stores[-1].start()
    for cp in stores:
        cp.wait()


def vmem(*shape, dtype=F32):
    return pltpu.VMEM(shape, dtype)


def body(resid, token_ids, code_proj, w_query, w_key, w_value, gain, out_grad):
    dma = pltpu.SemaphoreType.DMA
    any_spec = pl.BlockSpec(memory_space=pl.ANY)
    vm = pl.BlockSpec(memory_space=pltpu.VMEM)
    sds = jax.ShapeDtypeStruct
    scale = 1.0 / math.sqrt(T * lax.axis_size(ALL))
    w_out, resid_grad, gain_out, code_out = pl.pallas_call(
        functools.partial(kernel, scale),
        name="layer",
        out_shape=(sds((3, 16, 2 * HALF), F32), sds((T, D), BF16), sds((1, 2 * HALF), F32), sds((6, D), F32)),
        in_specs=[any_spec] * 8,
        out_specs=(vm, any_spec, vm, vm),
        scratch_shapes=[
            vmem(1, T, dtype=jnp.int32), vmem(6, D), vmem(1, 2 * HALF), dma((7,)),
            vmem(3, D, HALF, dtype=BF16), dma((3,)), vmem(2, T, D, dtype=BF16),
            vmem(8, T, DH, dtype=BF16), vmem(8, T, DH, dtype=BF16), vmem(8, T, DH, dtype=BF16),
            vmem(16, T, DH), vmem(16, T, DH), vmem(8, T, DH, dtype=BF16), dma((8,)),
            vmem(8, T, T, dtype=BF16), vmem(8, T, DH, dtype=BF16),
            vmem(16, T), vmem(16, T), vmem(2, 16, T, dtype=BF16), vmem(3, 16, D, dtype=BF16), vmem(8, 1, DH),
            dma((8,)), dma((8,)), dma((2,)), dma((2,)), pltpu.SemaphoreType.REGULAR,
            vmem(2, 2, 4, DH, DH), vmem(2, 16, 32, DH), vmem(2, 16, 32, DH), vmem(2, 16, 32, DH), vmem(2, 16, 32, DH),
            dma((6, 15)), dma((6, 15)),
            vmem(4, 4, 2, 4, 16, 2 * T, dtype=BF16), vmem(6, 2 * T, 256, dtype=BF16), dma((2,)),
            vmem(4, 8, D), vmem(3, 8, D), dma((2, 3)),
            vmem(16, 8, DH), vmem(16, 8, DH), vmem(8, DH), vmem(16, 8, DH),
            vmem(6, 2, 4, 16, 256), dma((2, 6, 2, 4)), dma,
            dma((2, 6, 2, 3)),
            *[vmem(2, *DIMS[a], 16, 256) for a, _ in PLAN],
            *[vmem(*DIMS2[a], 16, 256) for a, _ in PLAN],
            *[vmem(*DIMS[a], 16, 256) for _ in range(3) for a, _ in PLAN],
            *[vmem(*DIMS2[a], 16, 256) for _ in range(3) for a, _ in PLAN],
        ],
        compiler_params=pltpu.CompilerParams(collective_id=0, has_side_effects=True, vmem_limit_bytes=67_043_328),
    )(token_ids, code_proj, gain[None], resid[0], out_grad[0], w_query, w_key, w_value)
    shapes = (sds((T, D), BF16), sds((3, 16, 2 * HALF), F32), sds((1, 2 * HALF), F32), sds((6, D), F32))
    resid_grad, w_out, gain_out, code_out = pl.pallas_call(
        hand_over,
        name="hand_over",
        out_shape=shapes,
        in_specs=[any_spec] * 4,
        out_specs=[any_spec] * 4,
        scratch_shapes=[*[vmem(*n.shape, dtype=n.dtype) for n in shapes], dma((2, 7))],
    )(resid_grad, w_out, gain_out, code_out)
    return resid_grad[None], w_out.transpose(1, 0, 2), gain_out[0], code_out


def solution(mesh):
    finer = Mesh(mesh.devices.reshape(4, 4, 2, 4), ALL)
    seq = ("z", "y", "c")
    return jax.shard_map(
        body,
        mesh=finer,
        in_specs=(P("x", seq, None), P("x", seq), P(), P(), P(), P(), P(), P("x", seq, None)),
        out_specs=(P("x", seq, None), P(ALL, None, None), P(), P()),
        check_vma=False,
    )
```

```python
import functools
import math

import jax
import jax.numpy as jnp
from jax import lax
from jax.experimental import pallas as pl
from jax.experimental.pallas import tpu as pltpu
from jax.sharding import Mesh
from jax.sharding import PartitionSpec as P

HEADS = 8
DH = 128
T = 512
D = 2048
HALF = 512
ALL = ("z", "y", "c", "x")
MESH = pl.DeviceIdType.MESH
F32 = jnp.float32
BF16 = jnp.bfloat16

fsq_levels = (8, 8, 8, 5, 5, 5)
fsq_bases = (1, 8, 64, 512, 2560, 12800)

NT = (((1,), (1,)), ((), ()))
TN = (((0,), (0,)), ((), ()))


def dot(a, b, dims=None):
    if dims is None:
        return jnp.dot(a, b, preferred_element_type=F32)
    return lax.dot_general(a, b, dims, preferred_element_type=F32)


def entry_signal(devices):
    barrier = pltpu.get_barrier_semaphore()
    for device in devices:
        pl.semaphore_signal(barrier, inc=1, device_id=device, device_id_type=MESH)
    return lambda: pl.semaphore_wait(barrier, len(devices))


def send(src, dst, ssem, rsem, device):
    copy = pltpu.make_async_remote_copy(
        src_ref=src, dst_ref=dst, send_sem=ssem, recv_sem=rsem, device_id=device, device_id_type=MESH
    )
    copy.start()
    return copy


def ring(axis, step):
    return lax.rem(lax.axis_index(axis) + step, 4)


PLAN = (("x", 1), ("x", -1), ("y", 1), ("z", 1), ("y", -1), ("z", -1))
ORDER = {"x": ("x", "z", "y"), "y": ("y", "x", "z"), "z": ("z", "y", "x")}
DIMS = {"x": (4, 4, 2), "y": (4, 2, 4), "z": (4, 2, 4)}
DIMS2 = {"x": (4, 2), "y": (4, 2), "z": (2, 4)}


class Trace:
    on = False
    scope = None

    def __call__(self, name=None):
        if not self.on:
            return
        if self.scope is not None:
            self.scope.__exit__(None, None, None)
        self.scope = jax.named_scope(name) if name else None
        if name:
            self.scope.__enter__()


def kernel(
    scale, ids_hbm, proj_hbm, gain_hbm, resid_hbm, og_hbm, wq_hbm, wk_hbm, wv_hbm,
    wout, rg_hbm, gain_out, code_out,
    ids_ref, proj_ref, gain_ref, opsem, wbuf, wsem, xb, q, k, v, sqk, dkv, og, ogsem, sc, datt, nf, ns, nall, proj3, gain_row,
    xssem, xrsem, gsem, nsem, free_sem,
    blk, pre, sbuf, rbuf, obuf, sssem, srsem,
    xt_ref, g_ref, igsem, ar, arr, arsem, asend, agot, asum, aall, got, gotsem, rgsem, sems, *scr,
):
    tr = Trace()

    def pairs(first, last, step, width=2):
        def several(i, _):
            for n in range(width):
                step(width * i + n)
            return 0

        lax.fori_loop(first // width, last // width, several, 0)

    tx, t2 = scr[0:6], scr[6:12]
    recv = [[scr[12 + 18 * phase + 6 * m : 18 + 18 * phase + 6 * m] for m in range(3)] for phase in range(2)]
    c = lax.axis_index("c")
    peer = {"c": 1 - c}
    y = lax.axis_index("y")
    z = lax.axis_index("z")
    own_col = pl.multiple_of(c * HALF, HALF)
    peer_col = pl.multiple_of((1 - c) * HALF, HALF)
    mine = c * 4
    other = (1 - c) * 4

    tr("enter")
    small_loads = []
    for n, (src, dst) in enumerate(((ids_hbm, ids_ref), (proj_hbm, proj_ref), (gain_hbm, gain_ref))):
        small_loads.append(pltpu.make_async_copy(src, dst, opsem.at[n]))
        small_loads[-1].start()
    xloads = []
    for n in range(4):
        cols = pl.ds(n * 512, 512)
        xloads.append(pltpu.make_async_copy(resid_hbm.at[:, cols], xb.at[0, :, cols], opsem.at[3 + n]))
        xloads[-1].start()
    loads = [
        pltpu.make_async_copy(w.at[:, pl.ds(own_col, HALF)], wbuf.at[n], wsem.at[n])
        for n, w in enumerate((wk_hbm, wv_hbm, wq_hbm))
    ]
    ogloads = []
    for h in range(4):
        for m, (first, col) in enumerate(((other, peer_col), (mine, own_col))):
            ogloads.append(pltpu.make_async_copy(
                og_hbm.at[:, pl.ds(pl.multiple_of(col + h * DH, DH), DH)], og.at[first + h], ogsem.at[m * 4 + h]))

    plane = [{"z": ring("z", dz), "y": ring("y", dy)} for dz in range(4) for dy in range(4) if dz or dy]
    plane += [{"x": ring("x", n)} for n in (1, 2, 3)] + [peer]
    plane += [{a: ring(a, n), "c": 1 - c} for a in ("x", "y", "z") for n in (1, 2, 3)]
    all_entered = entry_signal(plane)

    for cp in small_loads:
        cp.wait()
    ids = ids_ref[...].astype(F32)
    nf[...] = jnp.zeros_like(nf)
    rest = jnp.zeros((8, D), F32)
    row = lax.broadcasted_iota(jnp.int32, (8, 1), 0)
    inv_level = jnp.zeros((8, 1), F32)
    for j, (level, base) in enumerate(zip(fsq_levels, fsq_bases)):
        quot = jnp.floor((ids + 0.5) * (1.0 / base)) if base > 1 else ids
        digit = quot - level * jnp.floor((quot + 0.5) * (1.0 / level))
        nf[j : j + 1, :] = 2.0 * digit - (level - 1.0)
        inv_level = jnp.where(row == j, 1.0 / (level - 1.0), inv_level)
    proj3[...] = jnp.zeros_like(proj3)
    rest = proj_ref[...] * inv_level[0:6]
    for t in range(3):
        term = rest.astype(BF16)
        proj3[t, 0:6, :] = term
        rest = rest - term.astype(F32)
    nums = nf[...].astype(BF16)
    numt = jnp.concatenate([nums, nums, nums], axis=0)

    tr("inputs")
    xcopies = []
    for j in range(8):
        if j % 2 == 0:
            xloads[j // 2].wait()
        if j == 2:
            for cp in loads + ogloads:
                cp.start()
        cols = slice(j * 256, j * 256 + 256)
        add = dot(numt, proj3[:, :, cols].reshape(48, 256), TN)
        x = (xb[0, :, cols].astype(F32) + add).astype(BF16)
        xb[0, :, cols] = x
        src, dst = tx[2 + j % 4].at[j // 4], recv[0][1 + j // 4][2 + j % 4]
        src[...] = x.astype(F32).reshape(4, 2, 4, 16, 256)
        if j == 0:
            all_entered()
        xcopies.append(send(src, dst, xssem.at[j], xrsem.at[j], peer))
    for h in range(4):
        ogloads[2 * h].wait()
        dkv[h] = og[other + h].astype(F32)
    g_copy = send(dkv.at[0:4], dkv.at[4:8], gsem.at[0], gsem.at[1], peer)
    n_copy = send(nf, ns, nsem.at[0], nsem.at[1], peer)

    def place(n, at, a):
        if n == 1:
            v[at] = a.astype(BF16)
        else:
            s = 1.0 / (1.0 + jnp.exp(-a))
            slope = s * (1.0 + a * (1.0 - s))
            if n == 0:
                k[at] = (a * s).astype(BF16)
                sqk[8 + at] = slope
            else:
                q[at] = (a * s).astype(BF16)
                sqk[at] = slope

    def project(slot, n, base):
        for half in range(2):
            p = dot(xb[slot], wbuf[n, :, half * 256 : half * 256 + 256])
            for hh in range(2):
                place(n, base + half * 2 + hh, p[:, hh * DH : hh * DH + DH])

    def kv_step(n):
        blk[0, n // 4, lax.rem(n, 4)] = dot(k[n], v[n], TN)

    def kv_steps(base):
        for h in range(4):
            kv_step(base + h)

    tr("own_proj")
    for n in range(2):
        loads[n].wait()
        project(0, n, mine)
    kv_steps(mine)
    for h in range(4):
        ogloads[2 * h + 1].wait()
    tr("peer_kv")
    for part in range(2):
        for j in range(4 * part, 4 * part + 4):
            xcopies[j].wait()
            xb[1, :, j * 256 : j * 256 + 256] = recv[0][1 + j // 4][2 + j % 4][...].reshape(512, 256).astype(BF16)
        ks = slice(part * 1024, part * 1024 + 1024)
        for n in range(2):
            for half in range(2):
                p = dot(xb[1, :, ks], wbuf[n, ks, half * 256 : half * 256 + 256])
                for hh in range(2):
                    a = p[:, hh * DH : hh * DH + DH]
                    h = half * 2 + hh
                    if part == 0:
                        dkv[8 + 4 * n + h] = a
                    else:
                        place(n, other + h, a + dkv[8 + 4 * n + h])

    me = z * 4 + y
    spots = sorted(((dz, dy) for dz in range(4) for dy in range(4) if dz or dy),
                   key=lambda o: -(min(o[0], 4 - o[0]) + min(o[1], 4 - o[1])))

    def to_all(src, dst, n):
        out = []
        for o, (dz, dy) in enumerate(spots):
            zt, yt = ring("z", dz), ring("y", dy)
            out.append(send(src.at[zt * 4 + yt], dst.at[me], sssem.at[n, o], srsem.at[n, o], {"z": zt, "y": yt}))
        return out

    def scan_start(s):
        sbuf[s] = (blk[s, 0] + blk[s, 1]).reshape(16, 32, DH)
        out = to_all(sbuf.at[s], rbuf.at[s], 2 * s)
        rbuf[s, me] = sbuf[s, me]
        return out

    def scan_middle(s, sent):
        for cp in sent:
            cp.wait()
        total = jnp.zeros((32, DH), F32)
        for i in range(16) if s == 0 else reversed(range(16)):
            obuf[s, i] = total
            total = total + rbuf[s, i]
        out = to_all(obuf.at[s], pre.at[s], 2 * s + 1)
        pre[s, me] = obuf[s, me]
        return out

    def scan_end(s, sent):
        for cp in sent:
            cp.wait()

    def state(s, b, h):
        base = pre[s, pl.ds(4 * h, 4)].reshape(DH, DH)
        if s == 0:
            return (base + jnp.where(b == 1, blk[0, 0, h], 0.0)).astype(BF16)
        return (base + jnp.where(b == 0, blk[1, 1, h], 0.0)).astype(BF16)

    tr("kv")
    kv_steps(other)
    sent = scan_start(0)
    tr("qproj")
    loads[2].wait()
    project(0, 2, mine)
    project(1, 2, other)
    g_copy.wait()
    for h in range(4):
        og[other + h] = dkv[4 + h].astype(BF16)
    n_copy.wait()
    nall[c] = nums
    nall[1 - c] = ns[...].astype(BF16)

    row_ids = lax.broadcasted_iota(jnp.int32, (T, T), 0)
    col_ids = lax.broadcasted_iota(jnp.int32, (T, T), 1)

    def score_step(n):
        s = jnp.where(col_ids <= row_ids, dot(q[n], k[n], NT), 0.0).astype(BF16)
        sc[n] = s
        dkv[8 + n] = dot(s, v[n])

    tr("scores1")
    pairs(0, 4, score_step)
    tr("scanmid0")
    sent = scan_middle(0, sent)
    tr("scores2")
    pairs(4, 8, score_step)

    def turn_step(n):
        cols = pl.ds(pl.multiple_of(n * 128, 128), 128)
        for slot in range(2):
            place = c if slot == 0 else 1 - c
            t = xb[slot, :, cols].T
            xt_ref[n // 4, lax.rem(n, 4), :, :, :, pl.ds(pl.multiple_of(place * T, T), T)] = t.reshape(2, 4, 16, T)

    tr("turn")
    pairs(0, 16, turn_step)
    tr("scanend0")
    scan_end(0, sent)

    def forward_step(n):
        b = n // 4
        h = lax.rem(n, 4)
        a = dkv[8 + n] + dot(q[n], state(0, b, h))
        g = og[n].astype(F32)
        dn = g * gain_ref[:, pl.ds(pl.multiple_of(c * HALF + h * DH, DH), DH)]
        square = jnp.sum(a * a, axis=-1, keepdims=True)
        cross = jnp.sum(dn * a, axis=-1, keepdims=True)
        inv = lax.rsqrt(square * (1.0 / DH) + 1e-06)
        normed = a * inv
        da = (dn * inv - normed * ((cross * inv) * (inv * (1.0 / DH)))).astype(BF16)
        datt[n] = da
        gain_row[n] = jnp.sum(g * normed, axis=0, keepdims=True)
        blk[1, b, h] = dot(q[n], da, TN)

    tr("fwd")
    pairs(0, 8, forward_step, 4)
    sent = scan_start(1)

    def put(kind, n, value):
        b = n // 4
        h = lax.rem(n, 4)
        g_ref[kind * 2 + h // 2, pl.ds(pl.multiple_of(b * T, T), T),
              pl.ds(pl.multiple_of(lax.rem(h, 2) * DH, DH), DH)] = value.astype(BF16)

    def back_step(i):
        n = lax.rem(i, 2) + 4 * lax.rem(i // 2, 2) + 2 * (i // 4)
        b = n // 4
        h = lax.rem(n, 4)
        da = datt[n]
        bs = jnp.where(col_ids <= row_ids, dot(da, v[n], NT), 0.0).astype(BF16)
        dq = dot(bs, k[n]) + dot(da, state(0, b, h), NT)
        put(0, n, dq * sqk[n])
        dkv[n] = dot(bs, q[n], TN)
        dkv[8 + n] = dot(sc[n], da, TN)

    def lhs(axis, i):
        if axis == "x":
            rows = xt_ref[:, :, :, i]
        elif axis == "y":
            rows = xt_ref[:, i]
        else:
            rows = xt_ref[i]
        return rows.reshape(512, 1024)

    def product(hp, i):
        axis = PLAN[hp][0]
        return dot(lhs(axis, i), g_ref[hp]).reshape(*DIMS[axis], 16, 256)

    sends = {}

    def go(hp, phase, m, src, dirn):
        axis = ORDER[PLAN[hp][0]][phase]
        sends[hp, phase, m] = send(src, recv[phase][m][hp], sems.at[0, hp, phase, m], sems.at[1, hp, phase, m],
                                   {axis: ring(axis, 1 if dirn == 1 else 3)})

    def far(hps):
        for hp in hps:
            tx[hp][0] = product(hp, ring(PLAN[hp][0], 2))
        for hp in hps:
            go(hp, 0, 0, tx[hp].at[0], PLAN[hp][1])

    def straight(hps):
        for hp in hps:
            axis, d = PLAN[hp]
            tx[hp][1] = product(hp, ring(axis, 3 if d == 1 else 1))
        for hp in hps:
            go(hp, 0, 1, tx[hp].at[1], -PLAN[hp][1])

    tr("back1")
    pairs(0, 4, back_step)
    far((0,))
    straight((0,))
    tr("scanmid1")
    sent = scan_middle(1, sent)
    tr("back2")
    pairs(4, 8, back_step)
    tr("xfirst")
    far((1,))
    straight((1,))
    tr("scanend1")
    scan_end(1, sent)

    def last_step(n):
        st = state(1, n // 4, lax.rem(n, 4))
        put(1, n, (dkv[n] + dot(v[n], st, NT)) * sqk[8 + n])
        put(2, n, dkv[8 + n] + dot(k[n], st))

    tr("last")
    pairs(0, 8, last_step, 4)
    pl.semaphore_signal(free_sem, inc=1, device_id=peer, device_id_type=MESH)
    tr("yzfirst")
    far((2, 3))
    far((4, 5))
    straight((2, 3, 4, 5))

    tr("small")
    smalls = []
    for t in range(3):
        parts = []
        for hp in (2 * t, 2 * t + 1):
            s = dot(nall[0], g_ref[hp, 0:T, :]) + dot(nall[1], g_ref[hp, T : 2 * T, :])
            s = s[0:8] * inv_level
            terms = []
            for _ in range(3):
                term = s.astype(BF16).astype(F32)
                s = s - term
                terms.append(term)
            terms.append(jnp.zeros_like(s))
            parts.append(jnp.concatenate(terms, axis=0))
        smalls.append(jnp.concatenate(parts, axis=1).astype(BF16))

    order_w = (2, 0, 1)

    def ig_tile(n, base, extra):
        total = None
        rows = pl.ds(pl.multiple_of(base, T), T)
        for t in range(3):
            left = jnp.concatenate([g_ref[2 * t, rows, :], g_ref[2 * t + 1, rows, :]], axis=1)
            if extra:
                left = jnp.concatenate([left, smalls[t]], axis=0)
            part = dot(left, wbuf[order_w[t], pl.ds(pl.multiple_of(n * 256, 256), 256), :], NT)
            total = part if total is None else total + part
        return total

    def ig_peer(n, _):
        total = ig_tile(n, (1 - c) * T, True)
        dkv[2 * n] = total[0:T, 0:DH]
        dkv[2 * n + 1] = total[0:T, DH : 2 * DH]
        code = total[T : T + 8] + total[T + 8 : T + 16] + total[T + 16 : T + 24]
        ar[0, :, pl.ds(pl.multiple_of(n * 256, 256), 256)] = code
        return 0

    tr("ig1")
    lax.fori_loop(0, 8, ig_peer, 0)
    ar[0, 6:7, :] = jnp.zeros((1, D), F32)
    for h in range(4):
        ar[0, 6:7, pl.ds(pl.multiple_of(c * HALF + h * DH, DH), DH)] = gain_row[h] + gain_row[4 + h]

    steps = (("c", 0), ("x", 0), ("x", 1))

    def small(n):
        axis, m = steps[n]
        i = lax.axis_index(axis)
        partner = 3 - i if m else i + 1 - 2 * lax.rem(i, 2)
        return send(ar.at[n], arr.at[n], arsem.at[0, n], arsem.at[1, n], {axis: partner})

    def small_next(n, cp):
        cp.wait()
        ar[n + 1] = ar[n] + arr[n]
        return small(n + 1) if n + 1 < 3 else None

    def plane_gather():
        for i in range(16):
            asend[i] = ar[3, :, i * 128 : i * 128 + 128]
        agot[me] = asend[me]
        return to_all(asend, agot, 4)

    def plane_return(sent):
        for cp in sent:
            cp.wait()
        total = agot[0]
        for i in range(1, 16):
            total = total + agot[i]
        asum[...] = total
        aall[me] = total
        out = []
        for o, (dz, dy) in enumerate(spots):
            out.append(send(asum, aall.at[me], sssem.at[5, o], srsem.at[5, o], {"z": ring("z", dz), "y": ring("y", dy)}))
        return out

    small_copy = small(0)
    pl.semaphore_wait(free_sem, 1)
    ig_copy = send(dkv, sqk, igsem.at[0], igsem.at[1], peer)

    def relay(hp):
        axis, d = PLAN[hp]
        mid = product(hp, ring(axis, 1 if d == 1 else 3))
        sends[hp, 0, 0].wait_recv()
        recv[0][0][hp][...] = recv[0][0][hp][...] + mid
        go(hp, 0, 2, recv[0][0][hp], d)

    tr("relay")
    small_copy = small_next(0, small_copy)
    for hp in (0, 1, 2, 3, 4, 5):
        relay(hp)
    tr("own")
    for hp in range(6):
        sends[hp, 0, 0].wait_send()
    for hp in range(6):
        tx[hp][0] = product(hp, ring(PLAN[hp][0], 0))

    tr("ig2")
    small_copy = small_next(1, small_copy)
    ig_copy.wait()

    def ig_own(n, _):
        total = ig_tile(n, c * T, False)
        total = total + jnp.concatenate([sqk[2 * n], sqk[2 * n + 1]], axis=1)
        xb[0, :, pl.ds(pl.multiple_of(n * 256, 256), 256)] = total.astype(BF16)
        return 0

    lax.fori_loop(0, 8, ig_own, 0)
    rg_copy = pltpu.make_async_copy(xb.at[0], rg_hbm, rgsem)
    rg_copy.start()

    def piece(hp, phase, i):
        axis = PLAN[hp][0]
        if phase == 1:
            return tx[hp].at[0, :, :, i] if axis == "y" else tx[hp].at[0, i]
        return t2[hp].at[:, i] if axis == "z" else t2[hp].at[i]

    def ends(hp, phase):
        sends[hp, phase, 1].wait_recv()
        sends[hp, phase, 2].wait_recv()
        return recv[phase][1][hp][...] + recv[phase][2][hp][...]

    def first(hp):
        go(hp, 1, 0, piece(hp, 1, ring(ORDER[PLAN[hp][0]][1], 2)), PLAN[hp][1])

    def second(hp):
        d = PLAN[hp][1]
        go(hp, 1, 1, piece(hp, 1, ring(ORDER[PLAN[hp][0]][1], 3 if d == 1 else 1)), -d)

    tr("ph1a")
    for hp in range(6):
        tx[hp][0] = tx[hp][0] + ends(hp, 0)
        first(hp)
        if hp == 1:
            second(0)
            second(1)
            small_next(2, small_copy)
            small_sent = plane_gather()
    for hp in range(2, 6):
        second(hp)
    tr("ph1b")
    for hp in range(6):
        axis, d = ORDER[PLAN[hp][0]][1], PLAN[hp][1]
        sends[hp, 1, 0].wait_recv()
        via = recv[1][0][hp]
        via[...] = via[...] + piece(hp, 1, ring(axis, 1 if d == 1 else 3))[...]
        go(hp, 1, 2, via, d)
    small_sent = plane_return(small_sent)
    tr("ph2a")
    for hp in range(6):
        prior, axis = ORDER[PLAN[hp][0]][1:]
        t2[hp][...] = piece(hp, 1, ring(prior, 0))[...] + ends(hp, 1)
        for m in (2, 1, 3, 0):
            for rel in (0, 1) if m else (1,):
                device = {axis: ring(axis, m), "c": c if rel == 0 else 1 - c} if m else peer
                if m and rel == 0:
                    device = {axis: ring(axis, m)}
                sends[hp, 2, (m, rel)] = send(
                    piece(hp, 2, ring(axis, m)).at[c if rel == 0 else 1 - c], got.at[hp, rel, m],
                    gotsem.at[0, hp, rel, m], gotsem.at[1, hp, rel, m], device)

    tr("final")
    for hp in range(6):
        for m in range(4):
            for rel in (0, 1) if m else (1,):
                sends[hp, 2, (m, rel)].wait_recv()
        last = ORDER[PLAN[hp][0]][2]
        own_sum = piece(hp, 2, ring(last, 0)).at[c][...] + got[hp, 0, 1] + got[hp, 0, 2] + got[hp, 0, 3]
        peer_sum = got[hp, 1, 0] + got[hp, 1, 1] + got[hp, 1, 2] + got[hp, 1, 3]
        shift = (hp % 2) * 256
        wout[hp // 2, :, pl.ds(pl.multiple_of(c * HALF + shift, 256), 256)] = own_sum * scale
        wout[hp // 2, :, pl.ds(pl.multiple_of((1 - c) * HALF + shift, 256), 256)] = peer_sum * scale
    for cp in small_sent:
        cp.wait()
    for i in range(16):
        code_out[:, i * 128 : i * 128 + 128] = aall[i, 0:6] * scale
        if i < 8:
            gain_out[:, i * 128 : i * 128 + 128] = aall[i, 6:7] * scale
    tr("drain")
    for (hp, phase, m), cp in sends.items():
        if (phase, m) != (0, 0):
            cp.wait_send()
    rg_copy.wait()
    tr()


def hand_over(*refs):
    ins, outs, bufs, sem = refs[:4], refs[4:8], refs[8:12], refs[12]
    parts = [(0, pl.ds(r * 128, 128)) for r in range(4)] + [(n, slice(None)) for n in (1, 2, 3)]
    loads = []
    for i, (n, rows) in enumerate(parts):
        loads.append(pltpu.make_async_copy(ins[n].at[rows], bufs[n].at[rows], sem.at[0, i]))
        loads[-1].start()
    stores = []
    for i, (n, rows) in enumerate(parts):
        loads[i].wait()
        stores.append(pltpu.make_async_copy(bufs[n].at[rows], outs[n].at[rows], sem.at[1, i]))
        stores[-1].start()
    for cp in stores:
        cp.wait()


def vmem(*shape, dtype=F32):
    return pltpu.VMEM(shape, dtype)


def body(resid, token_ids, code_proj, w_query, w_key, w_value, gain, out_grad):
    dma = pltpu.SemaphoreType.DMA
    any_spec = pl.BlockSpec(memory_space=pl.ANY)
    vm = pl.BlockSpec(memory_space=pltpu.VMEM)
    sds = jax.ShapeDtypeStruct
    scale = 1.0 / math.sqrt(T * lax.axis_size(ALL))
    w_out, resid_grad, gain_out, code_out = pl.pallas_call(
        functools.partial(kernel, scale),
        name="layer",
        out_shape=(sds((3, 16, 2 * HALF), F32), sds((T, D), BF16), sds((1, 2 * HALF), F32), sds((6, D), F32)),
        in_specs=[any_spec] * 8,
        out_specs=(vm, any_spec, vm, vm),
        scratch_shapes=[
            vmem(1, T, dtype=jnp.int32), vmem(6, D), vmem(1, 2 * HALF), dma((7,)),
            vmem(3, D, HALF, dtype=BF16), dma((3,)), vmem(2, T, D, dtype=BF16),
            vmem(8, T, DH, dtype=BF16), vmem(8, T, DH, dtype=BF16), vmem(8, T, DH, dtype=BF16),
            vmem(16, T, DH), vmem(16, T, DH), vmem(8, T, DH, dtype=BF16), dma((8,)),
            vmem(8, T, T, dtype=BF16), vmem(8, T, DH, dtype=BF16),
            vmem(16, T), vmem(16, T), vmem(2, 16, T, dtype=BF16), vmem(3, 16, D, dtype=BF16), vmem(8, 1, DH),
            dma((8,)), dma((8,)), dma((2,)), dma((2,)), pltpu.SemaphoreType.REGULAR,
            vmem(2, 2, 4, DH, DH), vmem(2, 16, 32, DH), vmem(2, 16, 32, DH), vmem(2, 16, 32, DH), vmem(2, 16, 32, DH),
            dma((6, 15)), dma((6, 15)),
            vmem(4, 4, 2, 4, 16, 2 * T, dtype=BF16), vmem(6, 2 * T, 256, dtype=BF16), dma((2,)),
            vmem(4, 8, D), vmem(3, 8, D), dma((2, 3)),
            vmem(16, 8, DH), vmem(16, 8, DH), vmem(8, DH), vmem(16, 8, DH),
            vmem(6, 2, 4, 16, 256), dma((2, 6, 2, 4)), dma,
            dma((2, 6, 2, 3)),
            *[vmem(2, *DIMS[a], 16, 256) for a, _ in PLAN],
            *[vmem(*DIMS2[a], 16, 256) for a, _ in PLAN],
            *[vmem(*DIMS[a], 16, 256) for _ in range(3) for a, _ in PLAN],
            *[vmem(*DIMS2[a], 16, 256) for _ in range(3) for a, _ in PLAN],
        ],
        compiler_params=pltpu.CompilerParams(collective_id=0, has_side_effects=True, vmem_limit_bytes=67_043_328),
    )(token_ids, code_proj, gain[None], resid[0], out_grad[0], w_query, w_key, w_value)
    shapes = (sds((T, D), BF16), sds((3, 16, 2 * HALF), F32), sds((1, 2 * HALF), F32), sds((6, D), F32))
    resid_grad, w_out, gain_out, code_out = pl.pallas_call(
        hand_over,
        name="hand_over",
        out_shape=shapes,
        in_specs=[any_spec] * 4,
        out_specs=[any_spec] * 4,
        scratch_shapes=[*[vmem(*n.shape, dtype=n.dtype) for n in shapes], dma((2, 7))],
    )(resid_grad, w_out, gain_out, code_out)
    return resid_grad[None], w_out.transpose(1, 0, 2), gain_out[0], code_out


def solution(mesh):
    finer = Mesh(mesh.devices.reshape(4, 4, 2, 4), ALL)
    seq = ("z", "y", "c")
    return jax.shard_map(
        body,
        mesh=finer,
        in_specs=(P("x", seq, None), P("x", seq), P(), P(), P(), P(), P(), P("x", seq, None)),
        out_specs=(P("x", seq, None), P(ALL, None, None), P(), P()),
        check_vma=False,
    )
```

```python
import functools
import math

import jax
import jax.numpy as jnp
from jax import lax
from jax.experimental import pallas as pl
from jax.experimental.pallas import tpu as pltpu
from jax.sharding import Mesh
from jax.sharding import PartitionSpec as P

HEADS = 8
DH = 128
T = 512
D = 2048
HALF = 512
ALL = ("z", "y", "c", "x")
MESH = pl.DeviceIdType.MESH
F32 = jnp.float32
BF16 = jnp.bfloat16

fsq_levels = (8, 8, 8, 5, 5, 5)
fsq_bases = (1, 8, 64, 512, 2560, 12800)

NT = (((1,), (1,)), ((), ()))
TN = (((0,), (0,)), ((), ()))


def dot(a, b, dims=None):
    if dims is None:
        return jnp.dot(a, b, preferred_element_type=F32)
    return lax.dot_general(a, b, dims, preferred_element_type=F32)


def entry_signal(devices):
    barrier = pltpu.get_barrier_semaphore()
    for device in devices:
        pl.semaphore_signal(barrier, inc=1, device_id=device, device_id_type=MESH)
    return lambda: pl.semaphore_wait(barrier, len(devices))


def send(src, dst, ssem, rsem, device):
    copy = pltpu.make_async_remote_copy(
        src_ref=src, dst_ref=dst, send_sem=ssem, recv_sem=rsem, device_id=device, device_id_type=MESH
    )
    copy.start()
    return copy


def ring(axis, step):
    return lax.rem(lax.axis_index(axis) + step, 4)


PLAN = (("x", 1), ("x", -1), ("y", 1), ("z", 1), ("y", -1), ("z", -1))
ORDER = {"x": ("x", "z", "y"), "y": ("y", "x", "z"), "z": ("z", "y", "x")}
DIMS = {"x": (4, 4, 2), "y": (4, 2, 4), "z": (4, 2, 4)}
DIMS2 = {"x": (4, 2), "y": (4, 2), "z": (2, 4)}


class Trace:
    on = False
    scope = None

    def __call__(self, name=None):
        if not self.on:
            return
        if self.scope is not None:
            self.scope.__exit__(None, None, None)
        self.scope = jax.named_scope(name) if name else None
        if name:
            self.scope.__enter__()


def kernel(
    scale, ids_hbm, proj_hbm, gain_hbm, resid_hbm, og_hbm, wq_hbm, wk_hbm, wv_hbm,
    wout, rg_hbm, gain_out, code_out,
    ids_ref, proj_ref, gain_ref, opsem, wbuf, wsem, xb, q, k, v, sqk, dkv, og, ogsem, sc, datt, nf, ns, nall, proj3, gain_row,
    xssem, xrsem, gsem, nsem, free_sem,
    blk, pre, sbuf, rbuf, obuf, sssem, srsem,
    xt_ref, g_ref, igsem, ar, arr, arsem, asend, agot, asum, aall, got, gotsem, rgsem, sems, *scr,
):
    tr = Trace()

    def pairs(first, last, step, width=2):
        def several(i, _):
            for n in range(width):
                step(width * i + n)
            return 0

        lax.fori_loop(first // width, last // width, several, 0)

    tx, t2 = scr[0:6], scr[6:12]
    recv = [[scr[12 + 18 * phase + 6 * m : 18 + 18 * phase + 6 * m] for m in range(3)] for phase in range(2)]
    c = lax.axis_index("c")
    peer = {"c": 1 - c}
    y = lax.axis_index("y")
    z = lax.axis_index("z")
    own_col = pl.multiple_of(c * HALF, HALF)
    peer_col = pl.multiple_of((1 - c) * HALF, HALF)
    mine = c * 4
    other = (1 - c) * 4

    tr("enter")
    small_loads = []
    for n, (src, dst) in enumerate(((ids_hbm, ids_ref), (proj_hbm, proj_ref), (gain_hbm, gain_ref))):
        small_loads.append(pltpu.make_async_copy(src, dst, opsem.at[n]))
        small_loads[-1].start()
    xloads = []
    for n in range(4):
        cols = pl.ds(n * 512, 512)
        xloads.append(pltpu.make_async_copy(resid_hbm.at[:, cols], xb.at[0, :, cols], opsem.at[3 + n]))
        xloads[-1].start()
    loads = [
        pltpu.make_async_copy(w.at[:, pl.ds(own_col, HALF)], wbuf.at[n], wsem.at[n])
        for n, w in enumerate((wk_hbm, wv_hbm, wq_hbm))
    ]
    ogloads = []
    for h in range(4):
        for m, (first, col) in enumerate(((other, peer_col), (mine, own_col))):
            ogloads.append(pltpu.make_async_copy(
                og_hbm.at[:, pl.ds(pl.multiple_of(col + h * DH, DH), DH)], og.at[first + h], ogsem.at[m * 4 + h]))

    plane = [{"z": ring("z", dz), "y": ring("y", dy)} for dz in range(4) for dy in range(4) if dz or dy]
    plane += [{"x": ring("x", n)} for n in (1, 2, 3)] + [peer]
    plane += [{a: ring(a, n), "c": 1 - c} for a in ("x", "y", "z") for n in (1, 2, 3)]
    all_entered = entry_signal(plane)

    for cp in small_loads:
        cp.wait()
    ids = ids_ref[...].astype(F32)
    nf[...] = jnp.zeros_like(nf)
    rest = jnp.zeros((8, D), F32)
    row = lax.broadcasted_iota(jnp.int32, (8, 1), 0)
    inv_level = jnp.zeros((8, 1), F32)
    for j, (level, base) in enumerate(zip(fsq_levels, fsq_bases)):
        quot = jnp.floor((ids + 0.5) * (1.0 / base)) if base > 1 else ids
        digit = quot - level * jnp.floor((quot + 0.5) * (1.0 / level))
        nf[j : j + 1, :] = 2.0 * digit - (level - 1.0)
        inv_level = jnp.where(row == j, 1.0 / (level - 1.0), inv_level)
    proj3[...] = jnp.zeros_like(proj3)
    rest = proj_ref[...] * inv_level[0:6]
    for t in range(3):
        term = rest.astype(BF16)
        proj3[t, 0:6, :] = term
        rest = rest - term.astype(F32)
    nums = nf[...].astype(BF16)
    numt = jnp.concatenate([nums, nums, nums], axis=0)

    tr("inputs")
    xcopies = []
    for j in range(8):
        if j % 2 == 0:
            xloads[j // 2].wait()
        if j == 2:
            for cp in loads + ogloads:
                cp.start()
        cols = slice(j * 256, j * 256 + 256)
        add = dot(numt, proj3[:, :, cols].reshape(48, 256), TN)
        x = (xb[0, :, cols].astype(F32) + add).astype(BF16)
        xb[0, :, cols] = x
        src, dst = tx[2 + j % 4].at[j // 4], recv[0][1 + j // 4][2 + j % 4]
        src[...] = x.astype(F32).reshape(4, 2, 4, 16, 256)
        if j == 0:
            all_entered()
        xcopies.append(send(src, dst, xssem.at[j], xrsem.at[j], peer))
    for h in range(4):
        ogloads[2 * h].wait()
        dkv[h] = og[other + h].astype(F32)
    g_copy = send(dkv.at[0:4], dkv.at[4:8], gsem.at[0], gsem.at[1], peer)
    n_copy = send(nf, ns, nsem.at[0], nsem.at[1], peer)

    def place(n, at, a):
        if n == 1:
            v[at] = a.astype(BF16)
        else:
            s = 1.0 / (1.0 + jnp.exp(-a))
            slope = s * (1.0 + a * (1.0 - s))
            if n == 0:
                k[at] = (a * s).astype(BF16)
                sqk[8 + at] = slope
            else:
                q[at] = (a * s).astype(BF16)
                sqk[at] = slope

    def project(slot, n, base):
        for half in range(2):
            p = dot(xb[slot], wbuf[n, :, half * 256 : half * 256 + 256])
            for hh in range(2):
                place(n, base + half * 2 + hh, p[:, hh * DH : hh * DH + DH])

    def kv_step(n):
        blk[0, n // 4, lax.rem(n, 4)] = dot(k[n], v[n], TN)

    def kv_steps(base):
        for h in range(4):
            kv_step(base + h)

    tr("own_proj")
    for n in range(2):
        loads[n].wait()
        project(0, n, mine)
    kv_steps(mine)
    for h in range(4):
        ogloads[2 * h + 1].wait()
    tr("peer_kv")
    for part in range(2):
        for j in range(4 * part, 4 * part + 4):
            xcopies[j].wait()
            xb[1, :, j * 256 : j * 256 + 256] = recv[0][1 + j // 4][2 + j % 4][...].reshape(512, 256).astype(BF16)
        ks = slice(part * 1024, part * 1024 + 1024)
        for n in range(2):
            for half in range(2):
                p = dot(xb[1, :, ks], wbuf[n, ks, half * 256 : half * 256 + 256])
                for hh in range(2):
                    a = p[:, hh * DH : hh * DH + DH]
                    h = half * 2 + hh
                    if part == 0:
                        dkv[8 + 4 * n + h] = a
                    else:
                        place(n, other + h, a + dkv[8 + 4 * n + h])

    me = z * 4 + y
    spots = sorted(((dz, dy) for dz in range(4) for dy in range(4) if dz or dy),
                   key=lambda o: -(min(o[0], 4 - o[0]) + min(o[1], 4 - o[1])))

    def to_all(src, dst, n):
        out = []
        for o, (dz, dy) in enumerate(spots):
            zt, yt = ring("z", dz), ring("y", dy)
            out.append(send(src.at[zt * 4 + yt], dst.at[me], sssem.at[n, o], srsem.at[n, o], {"z": zt, "y": yt}))
        return out

    def scan_start(s):
        sbuf[s] = (blk[s, 0] + blk[s, 1]).reshape(16, 32, DH)
        out = to_all(sbuf.at[s], rbuf.at[s], 2 * s)
        rbuf[s, me] = sbuf[s, me]
        return out

    def scan_middle(s, sent):
        for cp in sent:
            cp.wait()
        total = jnp.zeros((32, DH), F32)
        for i in range(16) if s == 0 else reversed(range(16)):
            obuf[s, i] = total
            total = total + rbuf[s, i]
        out = to_all(obuf.at[s], pre.at[s], 2 * s + 1)
        pre[s, me] = obuf[s, me]
        return out

    def scan_end(s, sent):
        for cp in sent:
            cp.wait()

    def state(s, b, h):
        base = pre[s, pl.ds(4 * h, 4)].reshape(DH, DH)
        if s == 0:
            return (base + jnp.where(b == 1, blk[0, 0, h], 0.0)).astype(BF16)
        return (base + jnp.where(b == 0, blk[1, 1, h], 0.0)).astype(BF16)

    tr("kv")
    kv_steps(other)
    sent = scan_start(0)
    tr("qproj")
    loads[2].wait()
    project(0, 2, mine)
    project(1, 2, other)
    g_copy.wait()
    for h in range(4):
        og[other + h] = dkv[4 + h].astype(BF16)
    n_copy.wait()
    nall[c] = nums
    nall[1 - c] = ns[...].astype(BF16)

    row_ids = lax.broadcasted_iota(jnp.int32, (T, T), 0)
    col_ids = lax.broadcasted_iota(jnp.int32, (T, T), 1)

    def score_step(n):
        s = jnp.where(col_ids <= row_ids, dot(q[n], k[n], NT), 0.0).astype(BF16)
        sc[n] = s
        dkv[8 + n] = dot(s, v[n])

    tr("scores1")
    pairs(0, 4, score_step)
    tr("scanmid0")
    sent = scan_middle(0, sent)
    tr("scores2")
    pairs(4, 8, score_step)

    def turn_step(n):
        cols = pl.ds(pl.multiple_of(n * 128, 128), 128)
        for slot in range(2):
            place = c if slot == 0 else 1 - c
            t = xb[slot, :, cols].T
            xt_ref[n // 4, lax.rem(n, 4), :, :, :, pl.ds(pl.multiple_of(place * T, T), T)] = t.reshape(2, 4, 16, T)

    tr("turn")
    pairs(0, 16, turn_step)
    tr("scanend0")
    scan_end(0, sent)

    def forward_step(n):
        b = n // 4
        h = lax.rem(n, 4)
        a = dkv[8 + n] + dot(q[n], state(0, b, h))
        g = og[n].astype(F32)
        dn = g * gain_ref[:, pl.ds(pl.multiple_of(c * HALF + h * DH, DH), DH)]
        square = jnp.sum(a * a, axis=-1, keepdims=True)
        cross = jnp.sum(dn * a, axis=-1, keepdims=True)
        inv = lax.rsqrt(square * (1.0 / DH) + 1e-06)
        normed = a * inv
        da = (dn * inv - normed * ((cross * inv) * (inv * (1.0 / DH)))).astype(BF16)
        datt[n] = da
        gain_row[n] = jnp.sum(g * normed, axis=0, keepdims=True)
        blk[1, b, h] = dot(q[n], da, TN)

    tr("fwd")
    pairs(0, 8, forward_step, 4)
    sent = scan_start(1)

    def put(kind, n, value):
        b = n // 4
        h = lax.rem(n, 4)
        g_ref[kind * 2 + h // 2, pl.ds(pl.multiple_of(b * T, T), T),
              pl.ds(pl.multiple_of(lax.rem(h, 2) * DH, DH), DH)] = value.astype(BF16)

    def back_step(i):
        n = lax.rem(i, 2) + 4 * lax.rem(i // 2, 2) + 2 * (i // 4)
        b = n // 4
        h = lax.rem(n, 4)
        da = datt[n]
        bs = jnp.where(col_ids <= row_ids, dot(da, v[n], NT), 0.0).astype(BF16)
        dq = dot(bs, k[n]) + dot(da, state(0, b, h), NT)
        put(0, n, dq * sqk[n])
        dkv[n] = dot(bs, q[n], TN)
        dkv[8 + n] = dot(sc[n], da, TN)

    def lhs(axis, i):
        if axis == "x":
            rows = xt_ref[:, :, :, i]
        elif axis == "y":
            rows = xt_ref[:, i]
        else:
            rows = xt_ref[i]
        return rows.reshape(512, 1024)

    def product(hp, i):
        axis = PLAN[hp][0]
        return dot(lhs(axis, i), g_ref[hp]).reshape(*DIMS[axis], 16, 256)

    sends = {}

    def go(hp, phase, m, src, dirn):
        axis = ORDER[PLAN[hp][0]][phase]
        sends[hp, phase, m] = send(src, recv[phase][m][hp], sems.at[0, hp, phase, m], sems.at[1, hp, phase, m],
                                   {axis: ring(axis, 1 if dirn == 1 else 3)})

    def far(hps):
        for hp in hps:
            tx[hp][0] = product(hp, ring(PLAN[hp][0], 2))
        for hp in hps:
            go(hp, 0, 0, tx[hp].at[0], PLAN[hp][1])

    def straight(hps):
        for hp in hps:
            axis, d = PLAN[hp]
            tx[hp][1] = product(hp, ring(axis, 3 if d == 1 else 1))
        for hp in hps:
            go(hp, 0, 1, tx[hp].at[1], -PLAN[hp][1])

    tr("back1")
    pairs(0, 4, back_step)
    far((0,))
    straight((0,))
    tr("scanmid1")
    sent = scan_middle(1, sent)
    tr("back2")
    pairs(4, 8, back_step)
    tr("xfirst")
    far((1,))
    straight((1,))
    tr("scanend1")
    scan_end(1, sent)

    def last_step(n):
        st = state(1, n // 4, lax.rem(n, 4))
        put(1, n, (dkv[n] + dot(v[n], st, NT)) * sqk[8 + n])
        put(2, n, dkv[8 + n] + dot(k[n], st))

    tr("last")
    pairs(0, 8, last_step, 4)
    pl.semaphore_signal(free_sem, inc=1, device_id=peer, device_id_type=MESH)
    tr("yzfirst")
    far((2, 3))
    far((4, 5))
    straight((2, 3, 4, 5))

    tr("small")
    smalls = []
    for t in range(3):
        parts = []
        for hp in (2 * t, 2 * t + 1):
            s = dot(nall[0], g_ref[hp, 0:T, :]) + dot(nall[1], g_ref[hp, T : 2 * T, :])
            s = s[0:8] * inv_level
            terms = []
            for _ in range(3):
                term = s.astype(BF16).astype(F32)
                s = s - term
                terms.append(term)
            terms.append(jnp.zeros_like(s))
            parts.append(jnp.concatenate(terms, axis=0))
        smalls.append(jnp.concatenate(parts, axis=1).astype(BF16))

    order_w = (2, 0, 1)

    def ig_tile(n, base, extra):
        total = None
        rows = pl.ds(pl.multiple_of(base, T), T)
        for t in range(3):
            left = jnp.concatenate([g_ref[2 * t, rows, :], g_ref[2 * t + 1, rows, :]], axis=1)
            if extra:
                left = jnp.concatenate([left, smalls[t]], axis=0)
            part = dot(left, wbuf[order_w[t], pl.ds(pl.multiple_of(n * 256, 256), 256), :], NT)
            total = part if total is None else total + part
        return total

    def ig_peer(n, _):
        total = ig_tile(n, (1 - c) * T, True)
        dkv[2 * n] = total[0:T, 0:DH]
        dkv[2 * n + 1] = total[0:T, DH : 2 * DH]
        code = total[T : T + 8] + total[T + 8 : T + 16] + total[T + 16 : T + 24]
        ar[0, :, pl.ds(pl.multiple_of(n * 256, 256), 256)] = code
        return 0

    tr("ig1")
    lax.fori_loop(0, 8, ig_peer, 0)
    ar[0, 6:7, :] = jnp.zeros((1, D), F32)
    for h in range(4):
        ar[0, 6:7, pl.ds(pl.multiple_of(c * HALF + h * DH, DH), DH)] = gain_row[h] + gain_row[4 + h]

    steps = (("c", 0), ("x", 0), ("x", 1))

    def small(n):
        axis, m = steps[n]
        i = lax.axis_index(axis)
        partner = 3 - i if m else i + 1 - 2 * lax.rem(i, 2)
        return send(ar.at[n], arr.at[n], arsem.at[0, n], arsem.at[1, n], {axis: partner})

    def small_next(n, cp):
        cp.wait()
        ar[n + 1] = ar[n] + arr[n]
        return small(n + 1) if n + 1 < 3 else None

    def plane_gather():
        for i in range(16):
            asend[i] = ar[3, :, i * 128 : i * 128 + 128]
        agot[me] = asend[me]
        return to_all(asend, agot, 4)

    def plane_return(sent):
        for cp in sent:
            cp.wait()
        total = agot[0]
        for i in range(1, 16):
            total = total + agot[i]
        asum[...] = total
        aall[me] = total
        out = []
        for o, (dz, dy) in enumerate(spots):
            out.append(send(asum, aall.at[me], sssem.at[5, o], srsem.at[5, o], {"z": ring("z", dz), "y": ring("y", dy)}))
        return out

    small_copy = small(0)
    pl.semaphore_wait(free_sem, 1)
    ig_copy = send(dkv, sqk, igsem.at[0], igsem.at[1], peer)

    def relay(hp):
        axis, d = PLAN[hp]
        mid = product(hp, ring(axis, 1 if d == 1 else 3))
        sends[hp, 0, 0].wait_recv()
        recv[0][0][hp][...] = recv[0][0][hp][...] + mid
        go(hp, 0, 2, recv[0][0][hp], d)

    tr("relay")
    small_copy = small_next(0, small_copy)
    for hp in (0, 1, 2, 3, 4, 5):
        relay(hp)
    tr("own")
    for hp in range(6):
        sends[hp, 0, 0].wait_send()
    for hp in range(6):
        tx[hp][0] = product(hp, ring(PLAN[hp][0], 0))

    tr("ig2")
    small_copy = small_next(1, small_copy)
    ig_copy.wait()

    def ig_own(n, _):
        total = ig_tile(n, c * T, False)
        total = total + jnp.concatenate([sqk[2 * n], sqk[2 * n + 1]], axis=1)
        xb[0, :, pl.ds(pl.multiple_of(n * 256, 256), 256)] = total.astype(BF16)
        return 0

    lax.fori_loop(0, 8, ig_own, 0)
    rg_copy = pltpu.make_async_copy(xb.at[0], rg_hbm, rgsem)
    rg_copy.start()

    def piece(hp, phase, i):
        axis = PLAN[hp][0]
        if phase == 1:
            return tx[hp].at[0, :, :, i] if axis == "y" else tx[hp].at[0, i]
        return t2[hp].at[:, i] if axis == "z" else t2[hp].at[i]

    def ends(hp, phase):
        sends[hp, phase, 1].wait_recv()
        sends[hp, phase, 2].wait_recv()
        return recv[phase][1][hp][...] + recv[phase][2][hp][...]

    def gather(hp, i):
        p = piece(hp, 1, i)
        two, three = ((r.at[:, :, i] if PLAN[hp][0] == "y" else r.at[i]) for r in (recv[0][1][hp], recv[0][2][hp]))
        p[...] = p[...] + two[...] + three[...]

    def first(hp):
        sends[hp, 0, 1].wait_recv()
        sends[hp, 0, 2].wait_recv()
        gather(hp, ring(ORDER[PLAN[hp][0]][1], 2))
        go(hp, 1, 0, piece(hp, 1, ring(ORDER[PLAN[hp][0]][1], 2)), PLAN[hp][1])

    def second(hp):
        d = PLAN[hp][1]
        gather(hp, ring(ORDER[PLAN[hp][0]][1], 3 if d == 1 else 1))
        go(hp, 1, 1, piece(hp, 1, ring(ORDER[PLAN[hp][0]][1], 3 if d == 1 else 1)), -d)

    tr("ph1a")
    for hp in range(6):
        first(hp)
        if hp == 1:
            second(0)
            second(1)
            small_next(2, small_copy)
            small_sent = plane_gather()
    for hp in range(2, 6):
        second(hp)
    tr("ph1b")
    for hp in range(6):
        axis, d = ORDER[PLAN[hp][0]][1], PLAN[hp][1]
        gather(hp, ring(axis, 1 if d == 1 else 3))
        gather(hp, ring(axis, 0))
        sends[hp, 1, 0].wait_recv()
        via = recv[1][0][hp]
        via[...] = via[...] + piece(hp, 1, ring(axis, 1 if d == 1 else 3))[...]
        go(hp, 1, 2, via, d)
    small_sent = plane_return(small_sent)
    tr("ph2a")
    for hp in range(6):
        prior, axis = ORDER[PLAN[hp][0]][1:]
        t2[hp][...] = piece(hp, 1, ring(prior, 0))[...] + ends(hp, 1)
        for m in (2, 1, 3, 0):
            for rel in (0, 1) if m else (1,):
                device = {axis: ring(axis, m), "c": c if rel == 0 else 1 - c} if m else peer
                if m and rel == 0:
                    device = {axis: ring(axis, m)}
                sends[hp, 2, (m, rel)] = send(
                    piece(hp, 2, ring(axis, m)).at[c if rel == 0 else 1 - c], got.at[hp, rel, m],
                    gotsem.at[0, hp, rel, m], gotsem.at[1, hp, rel, m], device)

    tr("final")
    for hp in range(6):
        for m in range(4):
            for rel in (0, 1) if m else (1,):
                sends[hp, 2, (m, rel)].wait_recv()
        last = ORDER[PLAN[hp][0]][2]
        own_sum = piece(hp, 2, ring(last, 0)).at[c][...] + got[hp, 0, 1] + got[hp, 0, 2] + got[hp, 0, 3]
        peer_sum = got[hp, 1, 0] + got[hp, 1, 1] + got[hp, 1, 2] + got[hp, 1, 3]
        shift = (hp % 2) * 256
        wout[hp // 2, :, pl.ds(pl.multiple_of(c * HALF + shift, 256), 256)] = own_sum * scale
        wout[hp // 2, :, pl.ds(pl.multiple_of((1 - c) * HALF + shift, 256), 256)] = peer_sum * scale
    for cp in small_sent:
        cp.wait()
    for i in range(16):
        code_out[:, i * 128 : i * 128 + 128] = aall[i, 0:6] * scale
        if i < 8:
            gain_out[:, i * 128 : i * 128 + 128] = aall[i, 6:7] * scale
    tr("drain")
    for (hp, phase, m), cp in sends.items():
        if (phase, m) != (0, 0):
            cp.wait_send()
    rg_copy.wait()
    tr()


def hand_over(*refs):
    ins, outs, bufs, sem = refs[:4], refs[4:8], refs[8:12], refs[12]
    parts = [(0, pl.ds(r * 128, 128)) for r in range(4)] + [(n, slice(None)) for n in (1, 2, 3)]
    loads = []
    for i, (n, rows) in enumerate(parts):
        loads.append(pltpu.make_async_copy(ins[n].at[rows], bufs[n].at[rows], sem.at[0, i]))
        loads[-1].start()
    stores = []
    for i, (n, rows) in enumerate(parts):
        loads[i].wait()
        stores.append(pltpu.make_async_copy(bufs[n].at[rows], outs[n].at[rows], sem.at[1, i]))
        stores[-1].start()
    for cp in stores:
        cp.wait()


def vmem(*shape, dtype=F32):
    return pltpu.VMEM(shape, dtype)


def body(resid, token_ids, code_proj, w_query, w_key, w_value, gain, out_grad):
    dma = pltpu.SemaphoreType.DMA
    any_spec = pl.BlockSpec(memory_space=pl.ANY)
    vm = pl.BlockSpec(memory_space=pltpu.VMEM)
    sds = jax.ShapeDtypeStruct
    scale = 1.0 / math.sqrt(T * lax.axis_size(ALL))
    w_out, resid_grad, gain_out, code_out = pl.pallas_call(
        functools.partial(kernel, scale),
        name="layer",
        out_shape=(sds((3, 16, 2 * HALF), F32), sds((T, D), BF16), sds((1, 2 * HALF), F32), sds((6, D), F32)),
        in_specs=[any_spec] * 8,
        out_specs=(vm, any_spec, vm, vm),
        scratch_shapes=[
            vmem(1, T, dtype=jnp.int32), vmem(6, D), vmem(1, 2 * HALF), dma((7,)),
            vmem(3, D, HALF, dtype=BF16), dma((3,)), vmem(2, T, D, dtype=BF16),
            vmem(8, T, DH, dtype=BF16), vmem(8, T, DH, dtype=BF16), vmem(8, T, DH, dtype=BF16),
            vmem(16, T, DH), vmem(16, T, DH), vmem(8, T, DH, dtype=BF16), dma((8,)),
            vmem(8, T, T, dtype=BF16), vmem(8, T, DH, dtype=BF16),
            vmem(16, T), vmem(16, T), vmem(2, 16, T, dtype=BF16), vmem(3, 16, D, dtype=BF16), vmem(8, 1, DH),
            dma((8,)), dma((8,)), dma((2,)), dma((2,)), pltpu.SemaphoreType.REGULAR,
            vmem(2, 2, 4, DH, DH), vmem(2, 16, 32, DH), vmem(2, 16, 32, DH), vmem(2, 16, 32, DH), vmem(2, 16, 32, DH),
            dma((6, 15)), dma((6, 15)),
            vmem(4, 4, 2, 4, 16, 2 * T, dtype=BF16), vmem(6, 2 * T, 256, dtype=BF16), dma((2,)),
            vmem(4, 8, D), vmem(3, 8, D), dma((2, 3)),
            vmem(16, 8, DH), vmem(16, 8, DH), vmem(8, DH), vmem(16, 8, DH),
            vmem(6, 2, 4, 16, 256), dma((2, 6, 2, 4)), dma,
            dma((2, 6, 2, 3)),
            *[vmem(2, *DIMS[a], 16, 256) for a, _ in PLAN],
            *[vmem(*DIMS2[a], 16, 256) for a, _ in PLAN],
            *[vmem(*DIMS[a], 16, 256) for _ in range(3) for a, _ in PLAN],
            *[vmem(*DIMS2[a], 16, 256) for _ in range(3) for a, _ in PLAN],
        ],
        compiler_params=pltpu.CompilerParams(collective_id=0, has_side_effects=True, vmem_limit_bytes=67_043_328),
    )(token_ids, code_proj, gain[None], resid[0], out_grad[0], w_query, w_key, w_value)
    shapes = (sds((T, D), BF16), sds((3, 16, 2 * HALF), F32), sds((1, 2 * HALF), F32), sds((6, D), F32))
    resid_grad, w_out, gain_out, code_out = pl.pallas_call(
        hand_over,
        name="hand_over",
        out_shape=shapes,
        in_specs=[any_spec] * 4,
        out_specs=[any_spec] * 4,
        scratch_shapes=[*[vmem(*n.shape, dtype=n.dtype) for n in shapes], dma((2, 7))],
    )(resid_grad, w_out, gain_out, code_out)
    return resid_grad[None], w_out.transpose(1, 0, 2), gain_out[0], code_out


def solution(mesh):
    finer = Mesh(mesh.devices.reshape(4, 4, 2, 4), ALL)
    seq = ("z", "y", "c")
    return jax.shard_map(
        body,
        mesh=finer,
        in_specs=(P("x", seq, None), P("x", seq), P(), P(), P(), P(), P(), P("x", seq, None)),
        out_specs=(P("x", seq, None), P(ALL, None, None), P(), P()),
        check_vma=False,
    )
```
